512 devices in a mesh: seq: 32 (over x, y, core), head: 16 (over z).
Axes of the slice: x: 4, y: 4, z: 16, core: 2. Of those that a mesh axis runs over, the one named last changes fastest.
Arguments:
- signal: bfloat16 [4096, 8192], P('seq', 'head'), may hold values from -6 to 6
- gate_input: bfloat16 [4096, 8192], P('seq', 'head'), may hold values from -6 to 6
- state_in: bfloat16 [4096, 128], P('seq'), may hold values from -1.796875 to 1.796875
- state_out: bfloat16 [4096, 128], P('seq'), may hold values from -1.796875 to 1.796875
- step_size: float32 [128, 4096], P('head', 'seq'), may hold values from 0 to 2, as said below
- log_decay: float32 [128, 4096], P('head', 'seq'), may hold values from -4 to 0, as said below
- skip_gain: float32 [128], P('head'), may hold values from 0.5 to 1.5
- norm_gain: float32 [8192], P('head'), may hold values from 0.1 to 1.9
- out_weight: bfloat16 [8192, 4096], P('head', 'seq'), may hold values from -0.125 to 0.125
Outputs:
- mixed: bfloat16 [4096, 4096], P('seq', 'head')
The draws below stay inside these ranges and needn't reach their ends.
Inputs may be any that keep to these rules, and one draw needn't show every extreme that they name: step_size is positive. log_decay is negative.
All inputs are finite; a program needn't handle non-finite values.
Results may differ from the reference program's by a relative error of at most 0.025.
Values may be sent and summed in bfloat16 or wider, within the bound.
A program may use at most 64 MiB of HBM per device.

```python
import math
import jax
import jax.numpy as jnp
from jax import lax

D = 4096
HEADS = 128
HEAD_DIM = 64
STATE = 128
SEQ = 4096
INNER = 8192
N_HEAD = 16


def head_rates(key):
    base = jax.random.fold_in(key, 7)
    pick = jax.random.uniform(jax.random.fold_in(base, 1), (HEADS,))
    slow_share = 0.5
    slow = jnp.exp(jax.random.uniform(jax.random.fold_in(base, 2), (HEADS,), jnp.float32, math.log(0.2 / SEQ), math.log(2.0 / SEQ)))
    fast = jnp.exp(jax.random.uniform(jax.random.fold_in(base, 3), (HEADS,), jnp.float32, math.log(1.0 / 50.0), math.log(1.0 / 8.0)))
    return jnp.where(pick < slow_share, slow, fast)


def draw_log_decay(key, part):
    decay_rates = head_rates(key)
    coarse_state = jax.random.uniform(jax.random.fold_in(key, 21), (HEADS, SEQ), jnp.float32, 0.5, 1.5)
    device_positions = jax.random.randint(jax.random.fold_in(key, 31), (4,), 0, SEQ)
    decay_amounts = jax.random.uniform(jax.random.fold_in(key, 41), (4,), jnp.float32, 0.2, 0.5)
    feature_column = jnp.arange(SEQ)[None, :]
    token_window = jnp.sum(jnp.where(feature_column == device_positions[:, None], jnp.log(1.0 - decay_amounts)[:, None], 0.0), axis=0)
    return (-decay_rates[:, None] * coarse_state + token_window[None, :]).astype(jnp.float32)


def draw_step_size(key, part):
    decay_rates = head_rates(key)
    ramp = 1.0 + 2.0 * jnp.arange(HEADS, dtype=jnp.float32) / max(HEADS - 1, 1)
    coarse_state = jax.random.uniform(jax.random.fold_in(key, 51), (HEADS, SEQ), jnp.float32, 0.5, 1.5)
    return (jnp.sqrt(decay_rates)[:, None] * ramp[:, None] * coarse_state).astype(jnp.float32)


def strengthened(values, stream_key, source, target, parts, factor):
    owner, partner = [(jnp.arange(values.shape[axis_at]) // (values.shape[axis_at] // parts)).reshape([-1 if axis == axis_at else 1 for axis in range(values.ndim)]) for axis_at in (source, target)]
    chosen = jax.random.permutation(stream_key, parts)[partner]
    strong = (owner == chosen) | (owner == (partner + parts // 2) % parts)
    return jnp.where(strong, factor * values, values)


def block_scale(key, dims, cuts, low, top_value):
    def one(position, blocks):
        heights = jax.random.uniform(jax.random.fold_in(jax.random.fold_in(key, 6), position), (blocks,), jnp.float32, low / len(cuts), top_value / len(cuts))
        return jnp.repeat(jnp.exp(heights), dims[position] // blocks).reshape((-1,) + (1,) * (len(dims) - position - 1))

    factor_of = one(*cuts[0])
    for cut in cuts[1:]:
        factor_of = factor_of * one(*cut)
    return factor_of


def centred(key, dims, deviation, most, split=(), kind=jnp.bfloat16):
    gain = block_scale(key, dims, split, -0.22, 0.18) if split else 1.0
    values = jax.random.normal(key, dims, jnp.float32) * deviation * gain
    return jnp.minimum(jnp.maximum(values, -most), most).astype(kind)


def noise_with(key, shape, scale, reach, shards, heavy, kind=jnp.bfloat16):
    array = scale * jax.random.normal(key, shape, jnp.float32)
    if shards:
        array = array * block_scale(key, shape, shards, -0.22, 0.18)
    return jnp.clip(strengthened(array, jax.random.fold_in(key, 3), *heavy), -reach, reach).astype(kind)


def setup_inputs(seed: int = 0) -> dict:
    keys = jax.random.split(jax.random.key(seed), 10)
    signal = centred(keys[0], (SEQ, INNER), 1.0, 6.0, ((0, 32), (1, 16)))
    gate_input = centred(keys[1], (SEQ, INNER), 1.0, 6.0, ((0, 32), (1, 16)))
    state_in = centred(keys[2], (SEQ, STATE), 0.3, 1.796875, ((0, 32),))
    state_out = centred(keys[3], (SEQ, STATE), 0.3, 1.796875, ((0, 32),))
    step_size = draw_step_size(jax.random.fold_in(keys[9], 71), 0)
    log_decay = draw_log_decay(jax.random.fold_in(keys[9], 71), 0)
    skip_gain = jnp.clip(0.5 + 1.0 * jax.random.uniform(keys[6], (HEADS,), jnp.float32) ** block_scale(keys[6], (HEADS,), ((0, 16),), -0.2, 0.2), 0.5, 1.5)
    norm_gain = jnp.clip(1.0 + 0.18 * jax.random.normal(keys[7], (INNER,), jnp.float32), 0.1, 1.9)
    out_weight = noise_with(keys[8], (INNER, D), INNER ** -0.5, 0.125, ((0, 16), (1, 32)), (0, 1, 32, 2.75))
    return dict(signal=signal, gate_input=gate_input, state_in=state_in, state_out=state_out, step_size=step_size, log_decay=log_decay, skip_gain=skip_gain, norm_gain=norm_gain, out_weight=out_weight)


HIGH = lax.Precision.HIGHEST

def ssd_block(state, inputs):
    signal_part, keys_part, queries_part, decay_part, step_sizes_local = inputs
    signal_f = signal_part.astype(jnp.float32)
    keys_f = keys_part.astype(jnp.float32)
    queries_f = queries_part.astype(jnp.float32)
    running = jnp.cumsum(decay_part, axis=1)
    width = decay_part.shape[1]
    lower = (jnp.arange(width)[:, None] >= jnp.arange(width)[None, :])[None]
    spread = running[:, :, None] - running[:, None, :]
    factors = jnp.where(lower, jnp.exp(jnp.where(lower, spread, 0.0)), 0.0)
    scores = jnp.dot(queries_f, keys_f.T, precision=HIGH)
    weights = factors * scores[None] * step_sizes_local[:, None, :]
    inside = jnp.einsum('hij,jhp->ihp', weights, signal_f, precision=HIGH)
    carried = jnp.einsum('in,hpn->ihp', queries_f, state, precision=HIGH) * jnp.exp(running).T[:, :, None]
    tail = jnp.exp(running[:, -1:] - running) * step_sizes_local
    fresh = jnp.einsum('hj,jhp,jn->hpn', tail, signal_f, keys_f, precision=HIGH)
    new_state = jnp.exp(running[:, -1])[:, None, None] * state + fresh
    return (new_state, inside + carried)

def reference(signal, gate_input, state_in, state_out, step_size, log_decay, skip_gain, norm_gain, out_weight):
    width = min(256, SEQ)
    blocks = SEQ // width
    inputs = (signal.reshape(blocks, width, HEADS, HEAD_DIM), state_in.reshape(blocks, width, STATE), state_out.reshape(blocks, width, STATE), log_decay.reshape(HEADS, blocks, width).transpose(1, 0, 2), step_size.reshape(HEADS, blocks, width).transpose(1, 0, 2))
    start = jnp.zeros((HEADS, HEAD_DIM, STATE), jnp.float32)
    final_state, outputs = lax.scan(ssd_block, start, inputs)
    channels = signal.reshape(SEQ, HEADS, HEAD_DIM).astype(jnp.float32)
    result = outputs.reshape(SEQ, HEADS, HEAD_DIM) + skip_gain[None, :, None] * channels
    gated = result.reshape(SEQ, HEADS * HEAD_DIM) * jax.nn.silu(gate_input.astype(jnp.float32))
    meansq = lax.optimization_barrier(jnp.mean(gated * gated, axis=1, keepdims=True))
    hidden = (gated * lax.rsqrt(meansq + 1e-05) * norm_gain[None, :]).astype(jnp.bfloat16)
    group_width = HEADS * HEAD_DIM // N_HEAD
    total = jnp.zeros((SEQ, D), jnp.float32)
    for group in range(N_HEAD):
        lo_edge = group * group_width
        partial_sum = jnp.dot(hidden[:, lo_edge:lo_edge + group_width], out_weight[lo_edge:lo_edge + group_width], preferred_element_type=jnp.float32).astype(jnp.bfloat16)
        partial_sum = lax.optimization_barrier(partial_sum)
        total = total + partial_sum.astype(jnp.float32)
    return total.astype(jnp.bfloat16)
```

```python
import jax
import jax.numpy as jnp
from jax import lax
from jax.experimental import pallas as pl
from jax.experimental.pallas import tpu as pltpu
from jax.sharding import PartitionSpec as P

MESH = pl.DeviceIdType.MESH
HIGH = lax.Precision.HIGHEST
F32 = jnp.float32
BF16 = jnp.bfloat16
NY = 4
NCHIP = 16
NZ = 16
RELAYS = (2, 4, 6)


def nt(a, b, precision=None):
    return lax.dot_general(
        a, b, (((1,), (1,)), ((), ())), precision=precision, preferred_element_type=F32
    )


def parent(j):
    return max(r for r in (0,) + RELAYS if r < j)


def iota(shape, dim):
    return lax.broadcasted_iota(jnp.int32, shape, dim)


def kernel(
    x_ref, z_ref, b_ref, c_ref, dt_ref, ld_ref, skip_ref, gain_ref, w_ref,
    out_ref,
    wbuf, sbuf, lbuf, pbuf, recva, retbuf, inbuf, incs, incall, hid, ssq, sendb, recvb, o2, osend,
    ylocal, gsil, expx_s,
    wl_sem, ws, wr, as_, ar, bs, br, ds, dr, rs_s, rs_r,
):
    s = lax.axis_index("seq")
    h = lax.axis_index("head")
    k = s // 2
    c = lax.rem(s, 2)
    cx = k // NY
    cy = lax.rem(k, NY)
    sib = (k * 2 + 1 - c, h)

    def chip(a, b):
        return lax.rem(cx + a, NY) * NY + lax.rem(cy + b, NY)

    offs = [(a, b) for a in range(NY) for b in range(NY) if (a, b) != (0, 0)]
    offs.sort(key=lambda o: -(min(o[0], NY - o[0]) + min(o[1], NY - o[1])))
    hops = sorted({j - parent(j) for j in range(1, NZ // 2 + 1)})
    zs = [d for a in hops for d in (a, NZ - a)]

    partners = [sib]
    partners += [(chip(a, b) * 2 + c, h) for a, b in offs]
    partners += [(s, lax.rem(h + d, NZ)) for d in zs]
    barrier = pltpu.get_barrier_semaphore()
    for p in partners:
        pl.semaphore_signal(barrier, inc=1, device_id=p, device_id_type=MESH)
    wl = pltpu.make_async_copy(w_ref, wbuf.at[k], wl_sem)
    wl.start()

    row = iota((128, 128), 0)
    col = iota((128, 128), 1)
    eye = (row == col).astype(F32)
    lower = row >= col
    ld = ld_ref[...]
    dt = dt_ref[...]
    run_c = nt(lower.astype(F32), ld, HIGH)
    run_r = nt(ld, lower.astype(F32), HIGH)
    dt_c = nt(eye, dt, HIGH)
    heads = (iota((8, 512), 1) // 64 == iota((8, 512), 0)).astype(F32)
    tail = jnp.exp(run_c[127:128, :] - run_c) * dt_c
    tailx = jnp.dot(tail, heads, precision=HIGH, preferred_element_type=F32)
    total = jnp.sum(run_r[:, 127:128] * heads, axis=0, keepdims=True)
    xf = x_ref[...].astype(F32)
    xt = (xf * tailx).astype(BF16)
    keys = b_ref[...]
    state = lax.dot_general(keys, xt, (((0,), (0,)), ((), ())), preferred_element_type=F32)
    for hf in range(2):
        sbuf[hf, 0:128, :] = state[:, 256 * hf : 256 * hf + 256]
        sbuf[hf, 128:136, :] = jnp.broadcast_to(total[:, 256 * hf : 256 * hf + 256], (8, 256))

    pl.semaphore_wait(barrier, len(partners))

    def to_sib(src, dst, n):
        return pltpu.make_async_remote_copy(
            src_ref=src, dst_ref=dst, send_sem=ds.at[n], recv_sem=dr.at[n],
            device_id=sib, device_id_type=MESH,
        )

    swap = to_sib(sbuf.at[1 - c], lbuf, 0)
    swap.start()

    nw = 0
    w_sent = []

    def send_w(src, kk, half, dest):
        nonlocal nw
        cp = pltpu.make_async_remote_copy(
            src_ref=src, dst_ref=wbuf.at[kk, pl.ds(256 * half, 256)],
            send_sem=ws.at[nw], recv_sem=wr.at[nw],
            device_id=(dest * 2 + c, h), device_id_type=MESH,
        )
        nw += 1
        cp.start()
        w_sent.append(cp)
        return cp

    def own_w(half):
        return w_ref.at[pl.ds(256 * half, 256)]

    first = []
    for d in (2, 1, 3):
        first.append((d, 0, send_w(own_w(0), k, 0, chip(0, d))))
        first.append((d, 1, send_w(own_w(1), k, 1, chip(d, 0))))
    late = []

    swap.wait()
    mine = sbuf[c]
    other = lbuf[...]
    early_own = jnp.full((1, 1), c, jnp.int32) == 0
    early = jnp.where(early_own, mine, other)
    later = jnp.where(early_own, other, mine)
    state_e = early[0:128]
    decay_e = early[128:129]
    decay_o = later[128:129]
    pair = (jnp.exp(decay_o) * state_e + later[0:128]).astype(BF16)
    decay_p = decay_e + decay_o
    hi = decay_p.astype(BF16).astype(F32)
    mid = (decay_p - hi).astype(BF16).astype(F32)
    low = decay_p - hi - mid
    r16 = iota((16, 256), 0)
    parts = jnp.where(r16 == 0, hi, jnp.where(r16 == 1, mid, jnp.where(r16 == 2, low, 0.0)))
    parts = parts.astype(BF16)
    for q in range(NCHIP):
        n0, l0 = 16 * (q % 8), 128 * (q // 8)
        pbuf[q, 0:16, :] = pair[n0 : n0 + 16, l0 : l0 + 128]
        pbuf[q, 16:32, :] = parts[:, l0 : l0 + 128]
    to_owner = []
    for n, (a, b) in enumerate(offs):
        q = chip(a, b)
        cp = pltpu.make_async_remote_copy(
            src_ref=pbuf.at[q], dst_ref=recva.at[k], send_sem=as_.at[n], recv_sem=ar.at[n],
            device_id=(q * 2 + c, h), device_id_type=MESH,
        )
        cp.start()
        to_owner.append(cp)
    recva[k] = pbuf[k]
    for d in (2, 1, 3):
        late.append(send_w(own_w(0), k, 0, chip(d, 0)))
        late.append(send_w(own_w(1), k, 1, chip(0, d)))

    queries = c_ref[...]
    scores = nt(queries, keys)
    lane = iota((128, 128), 1)
    expx_s[...] = jnp.dot(jnp.exp(run_c), heads, precision=HIGH, preferred_element_type=F32)
    for p in range(4):
        xp = x_ref[:, 128 * p : 128 * p + 128]
        ys = []
        for hh in (2 * p, 2 * p + 1):
            spread = run_c[:, hh : hh + 1] - run_r[hh : hh + 1, :]
            m = jnp.exp(jnp.where(lower, spread, -1e30)) * (scores * dt[hh : hh + 1, :])
            ys.append(jnp.dot(m.astype(BF16), xp, preferred_element_type=F32))
        skip = jnp.where(lane < 64, skip_ref[2 * p], skip_ref[2 * p + 1])
        ylocal[:, 128 * p : 128 * p + 128] = (
            jnp.where(lane < 64, ys[0], ys[1]) + skip * xp.astype(F32)
        )
    zf = z_ref[...].astype(F32)
    gsil[...] = zf / (1.0 + jnp.exp(-zf))

    for cp in to_owner:
        cp.wait_recv()
    carry = jnp.zeros((16, 128), F32)
    for kk in range(NCHIP):
        retbuf[kk] = carry.astype(BF16)
        m = recva[kk].astype(F32)
        carry = jnp.exp(m[16:17] + m[17:18] + m[18:19]) * carry + m[0:16]
    back = []
    for n, (a, b) in enumerate(offs):
        q = chip(a, b)
        cp = pltpu.make_async_remote_copy(
            src_ref=retbuf.at[q], dst_ref=inbuf.at[k], send_sem=bs.at[n], recv_sem=br.at[n],
            device_id=(q * 2 + c, h), device_id_type=MESH,
        )
        cp.start()
        back.append(cp)
    inbuf[k] = retbuf[k]
    for d, half, cp in first:
        cp.wait_recv()
        for e in (2, 1, 3):
            if half == 0:
                kk = chip(0, NY - d)
                late.append(send_w(wbuf.at[kk, pl.ds(0, 256)], kk, 0, chip(e, 0)))
            else:
                kk = chip(NY - d, 0)
                late.append(send_w(wbuf.at[kk, pl.ds(256, 256)], kk, 1, chip(0, e)))

    for cp in back:
        cp.wait_recv()
    incoming = jnp.concatenate(
        [inbuf[8 * i : 8 * i + 8].reshape(128, 128).astype(F32) for i in range(2)], axis=1
    )
    inc_odd = jnp.exp(decay_e) * incoming + state_e
    incs[...] = jnp.where(early_own, inc_odd, incoming).astype(BF16)
    swap2 = to_sib(incs, incall.at[c], 1)
    swap2.start()
    incall[c] = jnp.where(early_own, incoming, inc_odd).astype(BF16)
    swap2.wait()

    squares = jnp.zeros((8, 128), F32)
    gain = gain_ref[...]
    for hf in range(2):
        l0 = 256 * hf
        carried = jnp.dot(queries, incall[hf], preferred_element_type=F32)
        y = ylocal[:, l0 : l0 + 256] + carried * expx_s[:, l0 : l0 + 256]
        g = y * gsil[:, l0 : l0 + 256]
        squares = squares + nt(jnp.ones((8, 256), F32), g * g, HIGH)
        hid[c, :, l0 : l0 + 256] = (g * gain[:, l0 : l0 + 256]).astype(BF16)
    ssq[c] = squares
    swap3 = to_sib(hid.at[c], hid.at[c], 2)
    swap3.start()
    swap4 = to_sib(ssq.at[c], ssq.at[c], 3)
    swap4.start()
    wl.wait()
    for cp in late:
        cp.wait_recv()
    swap3.wait()
    swap4.wait()

    hidden = hid[...].reshape(256, 512)
    sums = [ssq[0, 0:1, :], ssq[1, 0:1, :]]
    slot = {}
    for side, most in ((0, 8), (1, 7)):
        for j in range(1, most + 1):
            slot[side, j] = len(slot)

    def children(side, j):
        return [i for i in range(j + 1, 9) if (side, i) in slot and parent(i) == j]

    def gather(dest, kids):
        part = jnp.dot(hidden, wbuf[dest], preferred_element_type=F32)
        sq = list(sums)
        for kid in kids:
            sent[kid].wait_recv()
            got = recvb[slot[kid]].astype(F32)
            part = part + got[0:256]
            sq = [sq[t] + got[256 + 2 * t : 257 + 2 * t] + got[257 + 2 * t : 258 + 2 * t] for t in (0, 1)]
        return part, sq

    sent = {}
    r16 = iota((16, 128), 0)
    for j in sorted(range(1, 9), key=lambda j: (j in RELAYS, -j)):
        for side in (0, 1):
            if (side, j) not in slot:
                continue
            n = slot[side, j]
            dest = lax.rem(h + (NZ - j if side == 0 else j), NZ)
            part, sq = gather(dest, [(side, i) for i in children(side, j)])
            sendb[n, 0:256, :] = part.astype(BF16)
            ext = jnp.zeros((16, 128), F32)
            for t in (0, 1):
                top = sq[t].astype(BF16).astype(F32)
                ext = jnp.where(r16 == 2 * t, top, jnp.where(r16 == 2 * t + 1, sq[t] - top, ext))
            sendb[n, 256:272, :] = ext.astype(BF16)
            a = j - parent(j)
            cp = pltpu.make_async_remote_copy(
                src_ref=sendb.at[n], dst_ref=recvb.at[n], send_sem=rs_s.at[n], recv_sem=rs_r.at[n],
                device_id=(s, lax.rem(h + (NZ - a if side == 0 else a), NZ)), device_id_type=MESH,
            )
            cp.start()
            sent[side, j] = cp

    part, sq = gather(h, [(side, i) for side in (0, 1) for i in children(side, 0)])

    r8 = iota((8, 128), 0)
    scale = [lax.rsqrt(v * (1.0 / 8192.0) + 1e-05) for v in sq]
    rows = jnp.where(r8 == 0, scale[0], jnp.where(r8 == 1, scale[1], 0.0))
    cols = nt(eye, rows, HIGH)
    t0 = part[0:128] * cols[:, 0:1]
    t1 = part[128:256] * cols[:, 1:2]
    osend[...] = jnp.where(early_own, t1, t0).astype(BF16)
    swap5 = to_sib(osend, o2.at[c], 4)
    swap5.start()
    o2[c] = jnp.where(early_own, t0, t1).astype(BF16)
    for cp in w_sent + to_owner + back + list(sent.values()):
        cp.wait_send()
    swap5.wait()
    out_ref[:, 0:128] = o2[0]
    out_ref[:, 128:256] = o2[1]


def body(
    signal, gate_input, state_in, state_out, step_size, log_decay, skip_gain, norm_gain, out_weight
):
    vmem = pl.BlockSpec(memory_space=pltpu.VMEM)
    dma = pltpu.SemaphoreType.DMA
    return pl.pallas_call(
        kernel,
        out_shape=jax.ShapeDtypeStruct((128, 256), BF16),
        in_specs=[vmem] * 6
        + [pl.BlockSpec(memory_space=pltpu.SMEM), vmem, pl.BlockSpec(memory_space=pl.ANY)],
        out_specs=vmem,
        scratch_shapes=[
            pltpu.VMEM((NCHIP, 512, 128), BF16),
            pltpu.VMEM((2, 136, 256), F32),
            pltpu.VMEM((136, 256), F32),
            pltpu.VMEM((NCHIP, 32, 128), BF16),
            pltpu.VMEM((NCHIP, 32, 128), BF16),
            pltpu.VMEM((NCHIP, 16, 128), BF16),
            pltpu.VMEM((NCHIP, 16, 128), BF16),
            pltpu.VMEM((128, 256), BF16),
            pltpu.VMEM((2, 128, 256), BF16),
            pltpu.VMEM((2, 128, 512), BF16),
            pltpu.VMEM((2, 8, 128), F32),
            pltpu.VMEM((15, 272, 128), BF16),
            pltpu.VMEM((15, 272, 128), BF16),
            pltpu.VMEM((2, 128, 128), BF16),
            pltpu.VMEM((128, 128), BF16),
            pltpu.VMEM((128, 512), F32),
            pltpu.VMEM((128, 512), F32),
            pltpu.VMEM((128, 512), F32),
            dma,
            dma((30,)), dma((30,)),
            dma((15,)), dma((15,)),
            dma((15,)), dma((15,)),
            dma((5,)), dma((5,)),
            dma((15,)), dma((15,)),
        ],
        compiler_params=pltpu.CompilerParams(
            collective_id=0, has_side_effects=True, vmem_limit_bytes=40 * 2**20
        ),
        name="ssd_layer",
    )(
        signal, gate_input, state_in, state_out, step_size, log_decay, skip_gain,
        norm_gain.reshape(1, -1), out_weight,
    )


def solution(mesh):
    in_specs = (
        P("seq", "head"),
        P("seq", "head"),
        P("seq", None),
        P("seq", None),
        P("head", "seq"),
        P("head", "seq"),
        P("head"),
        P("head"),
        P("head", "seq"),
    )
    out_specs = P("seq", "head")
    return jax.shard_map(body, mesh=mesh, in_specs=in_specs, out_specs=out_specs, check_vma=False)
```

```python
import jax
import jax.numpy as jnp
from jax import lax
from jax.experimental import pallas as pl
from jax.experimental.pallas import tpu as pltpu
from jax.sharding import PartitionSpec as P

MESH = pl.DeviceIdType.MESH
HIGH = lax.Precision.HIGHEST
F32 = jnp.float32
BF16 = jnp.bfloat16
NY = 4
NCHIP = 16
NZ = 16
RELAYS = (2, 4, 6)


def nt(a, b, precision=None):
    return lax.dot_general(
        a, b, (((1,), (1,)), ((), ())), precision=precision, preferred_element_type=F32
    )


def split3(v):
    hi = v.astype(BF16).astype(F32)
    mid = (v - hi).astype(BF16).astype(F32)
    return jnp.concatenate([hi, mid, v - hi - mid, jnp.zeros_like(v)], axis=0).astype(BF16)


def parent(j):
    return max(r for r in (0,) + RELAYS if r < j)


def iota(shape, dim):
    return lax.broadcasted_iota(jnp.int32, shape, dim)


def kernel(
    x_hbm, z_hbm, b_hbm, c_hbm, dt_hbm, ld_hbm, skip_hbm, gain_hbm, w_ref,
    out_ref,
    x_ref, z_ref, b_ref, c_ref, dt_ref, ld_ref, skip_ref, gain_ref,
    wbuf, sbuf, lbuf, pbuf, recva, retbuf, inbuf, incs, incall, hid, ssq, sendb, recvb, acc, o2, osend,
    ylocal, gsil, expx_s,
    ins, wl_sem, ws, wr, as_, ar, bs, br, ds, dr, rs_s, rs_r,
):
    s = lax.axis_index("seq")
    h = lax.axis_index("head")
    k = s // 2
    c = lax.rem(s, 2)
    cx = k // NY
    cy = lax.rem(k, NY)
    sib = (k * 2 + 1 - c, h)

    def chip(a, b):
        return lax.rem(cx + a, NY) * NY + lax.rem(cy + b, NY)

    offs = [(a, b) for a in range(NY) for b in range(NY) if (a, b) != (0, 0)]
    offs.sort(key=lambda o: -(min(o[0], NY - o[0]) + min(o[1], NY - o[1])))
    hops = sorted({j - parent(j) for j in range(1, NZ // 2 + 1)})
    zs = [d for a in hops for d in (a, NZ - a)]

    loads = []
    for n, (src, dst) in enumerate((
        (ld_hbm, ld_ref), (dt_hbm, dt_ref), (x_hbm, x_ref), (b_hbm, b_ref), (c_hbm, c_ref),
        (skip_hbm, skip_ref), (z_hbm, z_ref), (gain_hbm, gain_ref),
    )):
        cp = pltpu.make_async_copy(src, dst, ins.at[n])
        cp.start()
        loads.append(cp)

    partners = [sib]
    partners += [(chip(a, b) * 2 + c, h) for a, b in offs]
    partners += [(s, lax.rem(h + d, NZ)) for d in zs]
    barrier = pltpu.get_barrier_semaphore()
    for p in partners:
        pl.semaphore_signal(barrier, inc=1, device_id=p, device_id_type=MESH)
    wl = pltpu.make_async_copy(w_ref, wbuf.at[k], wl_sem)
    wl.start()

    row = iota((128, 128), 0)
    col = iota((128, 128), 1)
    eye = (row == col).astype(F32)
    lower = row >= col
    loads[0].wait()
    loads[1].wait()
    ld = ld_ref[...]
    dt = dt_ref[...]
    sums3 = nt(split3(ld), lower.astype(BF16))
    run_r = sums3[0:8] + sums3[8:16] + sums3[16:24]
    heads = (iota((8, 512), 1) // 64 == iota((8, 512), 0)).astype(F32)
    heads4 = (iota((32, 512), 1) // 64 == lax.rem(iota((32, 512), 0), 8)).astype(BF16)

    def expand(v):
        return lax.dot_general(
            split3(v), heads4, (((0,), (0,)), ((), ())), preferred_element_type=F32
        )

    total_h = run_r[:, 127:128]
    tailx = expand(jnp.exp(total_h - run_r) * dt)
    total = jnp.sum(total_h * heads, axis=0, keepdims=True)
    loads[2].wait()
    xf = x_ref[...].astype(F32)
    xt = (xf * tailx).astype(BF16)
    loads[3].wait()
    keys = b_ref[...]
    state = lax.dot_general(keys, xt, (((0,), (0,)), ((), ())), preferred_element_type=F32)
    for hf in range(2):
        sbuf[hf, 0:128, :] = state[:, 256 * hf : 256 * hf + 256]
        sbuf[hf, 128:136, :] = jnp.broadcast_to(total[:, 256 * hf : 256 * hf + 256], (8, 256))

    pl.semaphore_wait(barrier, len(partners))

    def to_sib(src, dst, n):
        return pltpu.make_async_remote_copy(
            src_ref=src, dst_ref=dst, send_sem=ds.at[n], recv_sem=dr.at[n],
            device_id=sib, device_id_type=MESH,
        )

    swap = to_sib(sbuf.at[1 - c], lbuf, 0)
    swap.start()

    nw = 0
    w_sent = []

    def send_w(src, kk, half, dest):
        nonlocal nw
        cp = pltpu.make_async_remote_copy(
            src_ref=src, dst_ref=wbuf.at[kk, pl.ds(256 * half, 256)],
            send_sem=ws.at[nw], recv_sem=wr.at[nw],
            device_id=(dest * 2 + c, h), device_id_type=MESH,
        )
        nw += 1
        cp.start()
        w_sent.append(cp)
        return cp

    def own_w(half):
        return w_ref.at[pl.ds(256 * half, 256)]

    first = []
    for d in (2, 1, 3):
        first.append((d, 0, send_w(own_w(0), k, 0, chip(0, d))))
        first.append((d, 1, send_w(own_w(1), k, 1, chip(d, 0))))
    late = []

    swap.wait()
    mine = sbuf[c]
    other = lbuf[...]
    early_own = jnp.full((1, 1), c, jnp.int32) == 0
    early = jnp.where(early_own, mine, other)
    later = jnp.where(early_own, other, mine)
    state_e = early[0:128]
    decay_e = early[128:129]
    decay_o = later[128:129]
    pair = (jnp.exp(decay_o) * state_e + later[0:128]).astype(BF16)
    decay_p = decay_e + decay_o
    hi = decay_p.astype(BF16).astype(F32)
    mid = (decay_p - hi).astype(BF16).astype(F32)
    low = decay_p - hi - mid
    r16 = iota((16, 256), 0)
    parts = jnp.where(r16 == 0, hi, jnp.where(r16 == 1, mid, jnp.where(r16 == 2, low, 0.0)))
    parts = parts.astype(BF16)
    for q in range(NCHIP):
        n0, l0 = 16 * (q % 8), 128 * (q // 8)
        pbuf[q, 0:16, :] = pair[n0 : n0 + 16, l0 : l0 + 128]
        pbuf[q, 16:32, :] = parts[:, l0 : l0 + 128]
    to_owner = []
    for n, (a, b) in enumerate(offs):
        q = chip(a, b)
        cp = pltpu.make_async_remote_copy(
            src_ref=pbuf.at[q], dst_ref=recva.at[k], send_sem=as_.at[n], recv_sem=ar.at[n],
            device_id=(q * 2 + c, h), device_id_type=MESH,
        )
        cp.start()
        to_owner.append(cp)
    recva[k] = pbuf[k]
    for d in (2, 1, 3):
        late.append(send_w(own_w(0), k, 0, chip(d, 0)))
        late.append(send_w(own_w(1), k, 1, chip(0, d)))

    for cp in loads[4:]:
        cp.wait()
    queries = c_ref[...]
    skip = jnp.dot(skip_ref[...], heads, precision=HIGH, preferred_element_type=F32)
    scores = nt(queries, keys)
    lane = iota((128, 128), 1)
    run_c = nt(lower.astype(F32), ld, HIGH)
    expx_s[...] = expand(jnp.exp(run_r))
    for p in range(4):
        xp = x_ref[:, 128 * p : 128 * p + 128]
        ys = []
        for hh in (2 * p, 2 * p + 1):
            spread = run_c[:, hh : hh + 1] - run_r[hh : hh + 1, :]
            m = jnp.exp(jnp.where(lower, spread, -1e30)) * (scores * dt[hh : hh + 1, :])
            ys.append(jnp.dot(m.astype(BF16), xp, preferred_element_type=F32))
        ylocal[:, 128 * p : 128 * p + 128] = (
            jnp.where(lane < 64, ys[0], ys[1])
            + skip[:, 128 * p : 128 * p + 128] * xp.astype(F32)
        )
    zf = z_ref[...].astype(F32)
    gsil[...] = zf / (1.0 + jnp.exp(-zf))

    for cp in to_owner:
        cp.wait_recv()
    carry = jnp.zeros((16, 128), F32)
    for kk in range(NCHIP):
        retbuf[kk] = carry.astype(BF16)
        m = recva[kk].astype(F32)
        carry = jnp.exp(m[16:17] + m[17:18] + m[18:19]) * carry + m[0:16]
    back = []
    for n, (a, b) in enumerate(offs):
        q = chip(a, b)
        cp = pltpu.make_async_remote_copy(
            src_ref=retbuf.at[q], dst_ref=inbuf.at[k], send_sem=bs.at[n], recv_sem=br.at[n],
            device_id=(q * 2 + c, h), device_id_type=MESH,
        )
        cp.start()
        back.append(cp)
    inbuf[k] = retbuf[k]
    for d, half, cp in first:
        cp.wait_recv()
        for e in (2, 1, 3):
            if half == 0:
                kk = chip(0, NY - d)
                late.append(send_w(wbuf.at[kk, pl.ds(0, 256)], kk, 0, chip(e, 0)))
            else:
                kk = chip(NY - d, 0)
                late.append(send_w(wbuf.at[kk, pl.ds(256, 256)], kk, 1, chip(0, e)))

    for cp in back:
        cp.wait_recv()
    incoming = jnp.concatenate(
        [inbuf[8 * i : 8 * i + 8].reshape(128, 128).astype(F32) for i in range(2)], axis=1
    )
    inc_odd = jnp.exp(decay_e) * incoming + state_e
    incs[...] = jnp.where(early_own, inc_odd, incoming).astype(BF16)
    swap2 = to_sib(incs, incall.at[c], 1)
    swap2.start()
    incall[c] = jnp.where(early_own, incoming, inc_odd).astype(BF16)
    swap2.wait()

    squares = jnp.zeros((8, 128), F32)
    gain = gain_ref[...]
    for hf in range(2):
        l0 = 256 * hf
        carried = jnp.dot(queries, incall[hf], preferred_element_type=F32)
        y = ylocal[:, l0 : l0 + 256] + carried * expx_s[:, l0 : l0 + 256]
        g = y * gsil[:, l0 : l0 + 256]
        squares = squares + nt(jnp.ones((8, 256), F32), g * g, HIGH)
        hid[c, :, l0 : l0 + 256] = (g * gain[:, l0 : l0 + 256]).astype(BF16)
    ssq[c] = squares
    swap3 = to_sib(hid.at[c], hid.at[c], 2)
    swap3.start()
    swap4 = to_sib(ssq.at[c], ssq.at[c], 3)
    swap4.start()
    wl.wait()
    for cp in late:
        cp.wait_recv()
    swap3.wait()
    swap4.wait()

    sides = {0: 8, 1: 7}
    slot = {}
    for side, most in sides.items():
        for j in range(1, most + 1):
            slot[side, j] = len(slot)
    halves = (1 - c, c)
    own_sq = [ssq[t, 0:1, :] for t in halves]
    r16 = iota((16, 128), 0)

    def target(side, j):
        return lax.rem(h + (NZ - j if side == 0 else j), NZ)

    def split_sq(v):
        top = v.astype(BF16).astype(F32)
        return jnp.where(r16 == 0, top, jnp.where(r16 == 1, v - top, 0.0)).astype(BF16)

    own_ext = [split_sq(v) for v in own_sq]
    sent = {}

    def send(side, j, t):
        n = slot[side, j]
        cp = pltpu.make_async_remote_copy(
            src_ref=sendb.at[n, t], dst_ref=recvb.at[n, t],
            send_sem=rs_s.at[n, t], recv_sem=rs_r.at[n, t],
            device_id=(s, target(side, j - parent(j))), device_id_type=MESH,
        )
        cp.start()
        sent[side, j, t] = cp

    def project(dest):
        wb = wbuf[dest]
        return [jnp.dot(hid[t], wb, preferred_element_type=F32) for t in halves]

    def leaf(side, j):
        n = slot[side, j]
        for t, part in enumerate(project(target(side, j))):
            sendb[n, t, 0:128, :] = part.astype(BF16)
            sendb[n, t, 128:144, :] = own_ext[t]

    def prepare(n, dest):
        for t, part in enumerate(project(dest)):
            acc[n, t] = part

    def gather(n, t, kids):
        part = acc[n, t]
        sq = own_sq[t]
        for side, i in kids:
            sent[side, i, t].wait_recv()
            got = recvb[slot[side, i], t].astype(F32)
            part = part + got[0:128]
            sq = sq + got[128:129] + got[129:130]
        return part, sq

    def relay(side, j, t):
        kids = [(side, i) for i in range(j + 1, sides[side] + 1) if parent(i) == j]
        part, sq = gather(RELAYS.index(j) * 2 + side, t, kids)
        n = slot[side, j]
        sendb[n, t, 0:128, :] = part.astype(BF16)
        sendb[n, t, 128:144, :] = split_sq(sq)
        send(side, j, t)

    both = (0, 1)
    for j in (8, 7):
        for side in both:
            if (side, j) in slot:
                leaf(side, j)
                send(side, j, 0)
    for j in (8, 7):
        for side in both:
            if (side, j) in slot:
                send(side, j, 1)
    for side in both:
        leaf(side, 5)
        send(side, 5, 0)
    for side in both:
        prepare(RELAYS.index(6) * 2 + side, target(side, 6))
    for side in both:
        leaf(side, 3)
        prepare(RELAYS.index(4) * 2 + side, target(side, 4))
    for j in (6, 4, 2):
        for t in (0, 1):
            for side in both:
                relay(side, j, t)
            for side in both:
                if t == 0:
                    send(side, j - 1, 1)
                elif j > 2:
                    send(side, j - 3, 0)
        if j == 6:
            for side in both:
                leaf(side, 1)
                prepare(RELAYS.index(2) * 2 + side, target(side, 2))
            prepare(2 * len(RELAYS), h)

    last = [(side, i) for side in both for i in (1, 2)]
    for t in (0, 1):
        part, sq = gather(2 * len(RELAYS), t, last)
        scale = lax.rsqrt(sq * (1.0 / 8192.0) + 1e-05)
        done = (part * jnp.broadcast_to(scale, (8, 128)).T[:, 0:1]).astype(BF16)
        if t == 0:
            osend[...] = done
            swap5 = to_sib(osend, o2.at[c], 4)
            swap5.start()
        else:
            o2[c] = done
    for cp in w_sent + to_owner + back + list(sent.values()):
        cp.wait_send()
    swap5.wait()
    out_ref[:, 0:128] = o2[0]
    out_ref[:, 128:256] = o2[1]


def body(
    signal, gate_input, state_in, state_out, step_size, log_decay, skip_gain, norm_gain, out_weight
):
    vmem = pl.BlockSpec(memory_space=pltpu.VMEM)
    dma = pltpu.SemaphoreType.DMA
    return pl.pallas_call(
        kernel,
        out_shape=jax.ShapeDtypeStruct((128, 256), BF16),
        in_specs=[pl.BlockSpec(memory_space=pltpu.HBM)] * 9,
        out_specs=vmem,
        scratch_shapes=[
            pltpu.VMEM((128, 512), BF16),
            pltpu.VMEM((128, 512), BF16),
            pltpu.VMEM((128, 128), BF16),
            pltpu.VMEM((128, 128), BF16),
            pltpu.VMEM((8, 128), F32),
            pltpu.VMEM((8, 128), F32),
            pltpu.VMEM((1, 8), F32),
            pltpu.VMEM((1, 512), F32),
            pltpu.VMEM((NCHIP, 512, 128), BF16),
            pltpu.VMEM((2, 136, 256), F32),
            pltpu.VMEM((136, 256), F32),
            pltpu.VMEM((NCHIP, 32, 128), BF16),
            pltpu.VMEM((NCHIP, 32, 128), BF16),
            pltpu.VMEM((NCHIP, 16, 128), BF16),
            pltpu.VMEM((NCHIP, 16, 128), BF16),
            pltpu.VMEM((128, 256), BF16),
            pltpu.VMEM((2, 128, 256), BF16),
            pltpu.VMEM((2, 128, 512), BF16),
            pltpu.VMEM((2, 8, 128), F32),
            pltpu.VMEM((15, 2, 144, 128), BF16),
            pltpu.VMEM((15, 2, 144, 128), BF16),
            pltpu.VMEM((7, 2, 128, 128), F32),
            pltpu.VMEM((2, 128, 128), BF16),
            pltpu.VMEM((128, 128), BF16),
            pltpu.VMEM((128, 512), F32),
            pltpu.VMEM((128, 512), F32),
            pltpu.VMEM((128, 512), F32),
            dma((8,)),
            dma,
            dma((30,)), dma((30,)),
            dma((15,)), dma((15,)),
            dma((15,)), dma((15,)),
            dma((5,)), dma((5,)),
            dma((15, 2)), dma((15, 2)),
        ],
        compiler_params=pltpu.CompilerParams(collective_id=0, has_side_effects=True),
        name="ssd_layer",
    )(
        signal, gate_input, state_in, state_out, step_size, log_decay,
        skip_gain.reshape(1, -1), norm_gain.reshape(1, -1), out_weight,
    )


def solution(mesh):
    in_specs = (
        P("seq", "head"),
        P("seq", "head"),
        P("seq", None),
        P("seq", None),
        P("head", "seq"),
        P("head", "seq"),
        P("head"),
        P("head"),
        P("head", "seq"),
    )
    out_specs = P("seq", "head")
    return jax.shard_map(body, mesh=mesh, in_specs=in_specs, out_specs=out_specs, check_vma=False)
```

```python
import jax
import jax.numpy as jnp
from jax import lax
from jax.experimental import pallas as pl
from jax.experimental.pallas import tpu as pltpu
from jax.sharding import PartitionSpec as P

MESH = pl.DeviceIdType.MESH
HIGH = lax.Precision.HIGHEST
F32 = jnp.float32
BF16 = jnp.bfloat16
NY = 4
NCHIP = 16
PRE = ()
POST = ((1, 0), (1, 1), (3, 0), (3, 1), (2, 0), (2, 1))
NZ = 16
RELAYS = (2, 4, 6)
ORDER = (
    "X8 X7 S81 S71 X5 P6 L3 P4 R60 S51 "
    "R61 S30 R40 S31 X1 P2 P0 R41 R20 S11 R21"
)


def nt(a, b, precision=None):
    return lax.dot_general(
        a, b, (((1,), (1,)), ((), ())), precision=precision, preferred_element_type=F32
    )


def split3(v):
    hi = v.astype(BF16).astype(F32)
    mid = (v - hi).astype(BF16).astype(F32)
    return jnp.concatenate([hi, mid, v - hi - mid, jnp.zeros_like(v)], axis=0).astype(BF16)


def parent(j):
    return max(r for r in (0,) + RELAYS if r < j)


def iota(shape, dim):
    return lax.broadcasted_iota(jnp.int32, shape, dim)


def kernel(
    x_hbm, z_hbm, b_hbm, c_hbm, dt_hbm, ld_hbm, skip_hbm, gain_hbm, w_ref,
    out_ref,
    x_ref, z_ref, b_ref, c_ref, dt_ref, ld_ref, skip_ref, gain_ref,
    wbuf, drow, dsib, lown, lsib, pbuf, recva, retbuf, inbuf, insib, hid, ssq, sendb, recvb, acc, o2, osend,
    ylocal, gsil, expx_s,
    ins, wl_sem, ws, wr, as_, ar, bs, br, ds, dr, rs_s, rs_r,
):
    s = lax.axis_index("seq")
    h = lax.axis_index("head")
    k = s // 2
    c = lax.rem(s, 2)
    cx = k // NY
    cy = lax.rem(k, NY)
    sib = (k * 2 + 1 - c, h)

    def chip(a, b):
        return lax.rem(cx + a, NY) * NY + lax.rem(cy + b, NY)

    offs = [(a, b) for a in range(NY) for b in range(NY) if (a, b) != (0, 0)]
    offs.sort(key=lambda o: -(min(o[0], NY - o[0]) + min(o[1], NY - o[1])))
    hops = sorted({j - parent(j) for j in range(1, NZ // 2 + 1)})
    zs = [d for a in hops for d in (a, NZ - a)]

    loads = []
    for n, (src, dst) in enumerate((
        (ld_hbm, ld_ref), (dt_hbm, dt_ref), (x_hbm, x_ref), (b_hbm, b_ref), (c_hbm, c_ref),
        (skip_hbm, skip_ref), (z_hbm, z_ref), (gain_hbm, gain_ref),
    )):
        cp = pltpu.make_async_copy(src, dst, ins.at[n])
        cp.start()
        loads.append(cp)

    partners = [sib]
    partners += [(chip(a, b) * 2 + c, h) for a, b in offs]
    partners += [(s, lax.rem(h + d, NZ)) for d in zs]
    barrier = pltpu.get_barrier_semaphore()
    for p in partners:
        pl.semaphore_signal(barrier, inc=1, device_id=p, device_id_type=MESH)
    wl = pltpu.make_async_copy(w_ref, wbuf.at[k], wl_sem)
    wl.start()

    row = iota((128, 128), 0)
    col = iota((128, 128), 1)
    eye = (row == col).astype(F32)
    lower = row >= col
    loads[0].wait()
    loads[1].wait()
    ld = ld_ref[...]
    dt = dt_ref[...]
    sums3 = nt(split3(ld), lower.astype(BF16))
    run_r = sums3[0:8] + sums3[8:16] + sums3[16:24]
    heads = (iota((8, 512), 1) // 64 == iota((8, 512), 0)).astype(F32)
    heads4 = (iota((32, 512), 1) // 64 == lax.rem(iota((32, 512), 0), 8)).astype(BF16)

    def expand(v):
        return lax.dot_general(
            split3(v), heads4, (((0,), (0,)), ((), ())), preferred_element_type=F32
        )

    total_h = run_r[:, 127:128]
    total = jnp.sum(total_h * heads, axis=0, keepdims=True)
    drow[...] = jnp.broadcast_to(total, (8, 512))

    def to_sib(src, dst, n):
        return pltpu.make_async_remote_copy(
            src_ref=src, dst_ref=dst, send_sem=ds.at[n], recv_sem=dr.at[n],
            device_id=sib, device_id_type=MESH,
        )

    tailx = expand(jnp.exp(total_h - run_r) * dt)
    loads[2].wait()
    xf = x_ref[...].astype(F32)
    xt = (xf * tailx).astype(BF16)
    loads[3].wait()
    keys = b_ref[...]
    state = lax.dot_general(keys, xt, (((0,), (0,)), ((), ())), preferred_element_type=F32)
    lown[...] = state.astype(BF16)
    pl.semaphore_wait(barrier, len(partners))

    swap = to_sib(drow, dsib, 0)
    swap.start()

    w_sent = []

    def w_copy(src, kk, half, dx, dy, dest):
        return pltpu.make_async_remote_copy(
            src_ref=src, dst_ref=wbuf.at[kk, pl.ds(256 * half, 256)],
            send_sem=ws.at[len(w_sent)], recv_sem=wr.at[half, NY * dx + dy],
            device_id=(dest * 2 + c, h), device_id_type=MESH,
        )

    def send_w(src, kk, half, dx, dy, dest):
        cp = w_copy(src, kk, half, dx, dy, dest)
        cp.start()
        w_sent.append(cp)

    def own_w(half):
        return w_ref.at[pl.ds(256 * half, 256)]

    def wait_w(half, kk, at):
        pltpu.make_async_remote_copy(
            src_ref=wbuf.at[kk, pl.ds(256 * half, 256)], dst_ref=wbuf.at[kk, pl.ds(256 * half, 256)],
            send_sem=ws.at[0], recv_sem=wr.at[half, at], device_id=sib, device_id_type=MESH,
        ).wait_recv()

    def pass_on(which):
        for d, half in which:
            if half == 0:
                kk = chip(0, NY - d)
                wait_w(0, kk, NY - d)
                for e in (2, 1, 3):
                    send_w(wbuf.at[kk, pl.ds(0, 256)], kk, 0, NY - e, NY - d, chip(e, 0))
            else:
                kk = chip(NY - d, 0)
                wait_w(1, kk, NY * (NY - d))
                for e in (2, 1, 3):
                    send_w(wbuf.at[kk, pl.ds(256, 256)], kk, 1, NY - d, NY - e, chip(0, e))

    for d in (2, 1, 3):
        send_w(own_w(0), k, 0, 0, NY - d, chip(0, d))
        send_w(own_w(1), k, 1, NY - d, 0, chip(d, 0))

    swap.wait()
    first_core = jnp.full((1, 1), c, jnp.int32) == 0
    d_sib = dsib[0:1, :]
    decay_p = total + d_sib
    pair = (state * jnp.where(first_core, jnp.exp(d_sib), 1.0)).astype(BF16)
    hi = decay_p.astype(BF16).astype(F32)
    mid = (decay_p - hi).astype(BF16).astype(F32)
    low = decay_p - hi - mid
    r16 = iota((16, 512), 0)
    parts = jnp.where(r16 == 0, hi, jnp.where(r16 == 1, mid, jnp.where(r16 == 2, low, 0.0)))
    parts = parts.astype(BF16)
    for q in range(NCHIP):
        n0, l0 = 32 * (q % 4), 128 * (q // 4)
        pbuf[q, 0:32, :] = pair[n0 : n0 + 32, l0 : l0 + 128]
        pbuf[q, 32:48, :] = parts[:, l0 : l0 + 128]
    to_owner = []
    for n, (a, b) in enumerate(offs):
        q = chip(a, b)
        cp = pltpu.make_async_remote_copy(
            src_ref=pbuf.at[q], dst_ref=recva.at[k], send_sem=as_.at[n], recv_sem=ar.at[n],
            device_id=(q * 2 + c, h), device_id_type=MESH,
        )
        cp.start()
        to_owner.append(cp)
    recva[k] = pbuf[k]
    swap1 = to_sib(lown, lsib, 1)
    swap1.start()
    for d in (2, 1, 3):
        send_w(own_w(0), k, 0, NY - d, 0, chip(d, 0))
        send_w(own_w(1), k, 1, 0, NY - d, chip(0, d))

    for cp in loads[4:]:
        cp.wait()
    queries = c_ref[...]
    skip = jnp.dot(skip_ref[...], heads, precision=HIGH, preferred_element_type=F32)
    scores = nt(queries, keys)
    lane = iota((128, 128), 1)
    run_c = nt(lower.astype(F32), ld, HIGH)
    expx_s[...] = expand(jnp.exp(run_r))
    for p in range(4):
        xp = x_ref[:, 128 * p : 128 * p + 128]
        ys = []
        for hh in (2 * p, 2 * p + 1):
            spread = run_c[:, hh : hh + 1] - run_r[hh : hh + 1, :]
            m = jnp.exp(jnp.where(lower, spread, -1e30)) * (scores * dt[hh : hh + 1, :])
            ys.append(jnp.dot(m.astype(BF16), xp, preferred_element_type=F32))
        ylocal[:, 128 * p : 128 * p + 128] = (
            jnp.where(lane < 64, ys[0], ys[1])
            + skip[:, 128 * p : 128 * p + 128] * xp.astype(F32)
        )
    zf = z_ref[...].astype(F32)
    gsil[...] = zf / (1.0 + jnp.exp(-zf))
    swap1.wait()
    other = jnp.dot(queries, lsib[...], preferred_element_type=F32)
    early_x = jnp.where(first_core, 1.0, jnp.exp(d_sib))
    ylocal[...] = ylocal[...] + expx_s[...] * jnp.where(first_core, 0.0, other)
    expx_s[...] = expx_s[...] * early_x

    pass_on(PRE)

    for cp in to_owner:
        cp.wait_recv()
    carry = jnp.zeros((32, 128), F32)
    for kk in range(NCHIP):
        retbuf[kk] = carry.astype(BF16)
        m = recva[kk].astype(F32)
        carry = jnp.exp(m[32:33] + m[33:34] + m[34:35]) * carry + m[0:32]
    back = []
    for n, (a, b) in enumerate(offs):
        q = chip(a, b)
        cp = pltpu.make_async_remote_copy(
            src_ref=retbuf.at[q], dst_ref=inbuf.at[k], send_sem=bs.at[n], recv_sem=br.at[n],
            device_id=(q * 2 + c, h), device_id_type=MESH,
        )
        cp.start()
        back.append(cp)
    inbuf[k] = retbuf[k]
    pass_on(POST)
    wl.wait()

    for cp in back:
        cp.wait_recv()
    swap2 = to_sib(inbuf, insib, 4)
    swap2.start()

    def carried(ref, p):
        part = ref[4 * p : 4 * p + 4].reshape(128, 128)
        return jnp.dot(queries, part, preferred_element_type=F32)

    for p in range(4):
        l0 = 128 * p
        ylocal[:, l0 : l0 + 128] = ylocal[:, l0 : l0 + 128] + (
            carried(inbuf, p) * expx_s[:, l0 : l0 + 128]
        )
    swap2.wait()

    squares = jnp.zeros((8, 128), F32)
    gain = gain_ref[...]
    for p in range(4):
        l0 = 128 * p
        y = ylocal[:, l0 : l0 + 128] + carried(insib, p) * expx_s[:, l0 : l0 + 128]
        g = y * gsil[:, l0 : l0 + 128]
        squares = squares + nt(jnp.ones((8, 128), F32), g * g, HIGH)
        hid[c, :, l0 : l0 + 128] = (g * gain[:, l0 : l0 + 128]).astype(BF16)
    ssq[c] = squares
    swap3 = to_sib(hid.at[c], hid.at[c], 2)
    swap3.start()
    swap4 = to_sib(ssq.at[c], ssq.at[c], 3)
    swap4.start()
    swap3.wait()
    swap4.wait()

    sides = {0: 8, 1: 7}
    slot = {}
    for side, most in sides.items():
        for j in range(1, most + 1):
            slot[side, j] = len(slot)
    halves = (1 - c, c)
    own_sq = [ssq[t, 0:1, :] for t in halves]
    r16 = iota((16, 128), 0)

    def target(side, j):
        return lax.rem(h + (NZ - j if side == 0 else j), NZ)

    def split_sq(sq):
        ext = jnp.zeros((16, 128), F32)
        for t, v in enumerate(sq):
            top = v.astype(BF16).astype(F32)
            ext = jnp.where(r16 == 2 * t, top, jnp.where(r16 == 2 * t + 1, v - top, ext))
        return ext.astype(BF16)

    own_ext = split_sq(own_sq)
    sent = {}

    def send(side, j, t):
        n = slot[side, j]
        rows = pl.ds(0, 128 if t else 144)
        cp = pltpu.make_async_remote_copy(
            src_ref=sendb.at[n, t, rows], dst_ref=recvb.at[n, t, rows],
            send_sem=rs_s.at[n, t], recv_sem=rs_r.at[n, t],
            device_id=(s, target(side, j - parent(j))), device_id_type=MESH,
        )
        cp.start()
        sent[side, j, t] = cp

    def project(dest):
        at = lax.rem(dest // NY - cx + NY, NY) * NY + lax.rem(lax.rem(dest, NY) - cy + NY, NY)

        for half in (0, 1):
            @pl.when(at >= NY if half == 0 else lax.rem(at, NY) > 0)
            def _(half=half):
                wait_w(half, dest, at)

        wb = wbuf[dest]
        return [jnp.dot(hid[t], wb, preferred_element_type=F32) for t in halves]

    def leaf(side, j):
        n = slot[side, j]
        for t, part in enumerate(project(target(side, j))):
            sendb[n, t, 0:128, :] = part.astype(BF16)
        sendb[n, 0, 128:144, :] = own_ext

    def prepare(n, dest):
        for t, part in enumerate(project(dest)):
            acc[n, t] = part

    def gather(n, t, kids):
        part = acc[n, t]
        sq = list(own_sq)
        for side, i in kids:
            sent[side, i, t].wait_recv()
            got = recvb[slot[side, i], t].astype(F32)
            part = part + got[0:128]
            for u in (0, 1):
                sq[u] = sq[u] + got[128 + 2 * u : 129 + 2 * u] + got[129 + 2 * u : 130 + 2 * u]
        return part, sq

    def relay(side, j, t):
        kids = [(side, i) for i in range(j + 1, sides[side] + 1) if parent(i) == j]
        part, sq = gather(RELAYS.index(j) * 2 + side, t, kids)
        n = slot[side, j]
        sendb[n, t, 0:128, :] = part.astype(BF16)
        if t == 0:
            sendb[n, 0, 128:144, :] = split_sq(sq)
        send(side, j, t)

    both = (0, 1)
    for step in ORDER.split():
        kind, j, t = step[0], int(step[1]), int(step[2:] or 0)
        if j == 0:
            prepare(2 * len(RELAYS), h)
            continue
        for side in both:
            if (side, j) not in slot:
                continue
            if kind == "P":
                prepare(RELAYS.index(j) * 2 + side, target(side, j))
            elif kind == "R":
                relay(side, j, t)
            else:
                if kind in "LX":
                    leaf(side, j)
                if kind in "SX":
                    send(side, j, t)

    last = [(side, i) for side in both for i in range(1, 9) if (side, i) in slot and parent(i) == 0]
    for t in (0, 1):
        part, sq = gather(2 * len(RELAYS), t, last)
        if t == 0:
            scale = [lax.rsqrt(v * (1.0 / 8192.0) + 1e-05) for v in sq]
            scale = [jnp.broadcast_to(v, (8, 128)).T[:, 0:1] for v in scale]
        done = (part * scale[t]).astype(BF16)
        if t == 0:
            osend[...] = done
            swap5 = to_sib(osend, o2.at[c], 5)
            swap5.start()
        else:
            o2[c] = done
    for cp in w_sent + to_owner + back + list(sent.values()):
        cp.wait_send()
    swap5.wait()
    out_ref[:, 0:128] = o2[0]
    out_ref[:, 128:256] = o2[1]


def body(
    signal, gate_input, state_in, state_out, step_size, log_decay, skip_gain, norm_gain, out_weight
):
    vmem = pl.BlockSpec(memory_space=pltpu.VMEM)
    args = [pltpu.with_memory_space_constraint(a, pltpu.HBM) for a in (
        signal, gate_input, state_in, state_out, step_size, log_decay,
        skip_gain.reshape(1, -1), norm_gain.reshape(1, -1), out_weight,
    )]
    dma = pltpu.SemaphoreType.DMA
    return pl.pallas_call(
        kernel,
        out_shape=jax.ShapeDtypeStruct((128, 256), BF16),
        in_specs=[pl.BlockSpec(memory_space=pltpu.HBM)] * 9,
        out_specs=vmem,
        scratch_shapes=[
            pltpu.VMEM((128, 512), BF16),
            pltpu.VMEM((128, 512), BF16),
            pltpu.VMEM((128, 128), BF16),
            pltpu.VMEM((128, 128), BF16),
            pltpu.VMEM((8, 128), F32),
            pltpu.VMEM((8, 128), F32),
            pltpu.VMEM((1, 8), F32),
            pltpu.VMEM((1, 512), F32),
            pltpu.VMEM((NCHIP, 512, 128), BF16),
            pltpu.VMEM((8, 512), F32),
            pltpu.VMEM((8, 512), F32),
            pltpu.VMEM((128, 512), BF16),
            pltpu.VMEM((128, 512), BF16),
            pltpu.VMEM((NCHIP, 48, 128), BF16),
            pltpu.VMEM((NCHIP, 48, 128), BF16),
            pltpu.VMEM((NCHIP, 32, 128), BF16),
            pltpu.VMEM((NCHIP, 32, 128), BF16),
            pltpu.VMEM((NCHIP, 32, 128), BF16),
            pltpu.VMEM((2, 128, 512), BF16),
            pltpu.VMEM((2, 8, 128), F32),
            pltpu.VMEM((15, 2, 144, 128), BF16),
            pltpu.VMEM((15, 2, 144, 128), BF16),
            pltpu.VMEM((7, 2, 128, 128), F32),
            pltpu.VMEM((2, 128, 128), BF16),
            pltpu.VMEM((128, 128), BF16),
            pltpu.VMEM((128, 512), F32),
            pltpu.VMEM((128, 512), F32),
            pltpu.VMEM((128, 512), F32),
            dma((8,)),
            dma,
            dma((30,)), dma((2, 16)),
            dma((15,)), dma((15,)),
            dma((15,)), dma((15,)),
            dma((6,)), dma((6,)),
            dma((15, 2)), dma((15, 2)),
        ],
        compiler_params=pltpu.CompilerParams(
            collective_id=0, has_side_effects=True, vmem_limit_bytes=40 * 2**20
        ),
        name="ssd_layer",
    )(*args)


def solution(mesh):
    in_specs = (
        P("seq", "head"),
        P("seq", "head"),
        P("seq", None),
        P("seq", None),
        P("head", "seq"),
        P("head", "seq"),
        P("head"),
        P("head"),
        P("head", "seq"),
    )
    out_specs = P("seq", "head")
    return jax.shard_map(body, mesh=mesh, in_specs=in_specs, out_specs=out_specs, check_vma=False)
```

```python
import jax
import jax.numpy as jnp
from jax import lax
from jax.experimental import pallas as pl
from jax.experimental.pallas import tpu as pltpu
from jax.sharding import PartitionSpec as P

MESH = pl.DeviceIdType.MESH
HIGH = lax.Precision.HIGHEST
F32 = jnp.float32
BF16 = jnp.bfloat16
NY = 4
NCHIP = 16
PASSED = ((2, 0), (2, 1), (1, 0), (1, 1), (3, 0), (3, 1))
NZ = 16
RELAYS = (2, 4, 6)
ORDER = (
    "X8", "X7", "S81", "S71", "X5", "P6", "R60", "S51",
    "R61", "X3", "P4", "R40", "S31", "R41", "X1", "P2",
    "R20", "S11", "R21", "P0",
)


def nt(a, b, precision=None):
    return lax.dot_general(
        a, b, (((1,), (1,)), ((), ())), precision=precision, preferred_element_type=F32
    )


def split3(v):
    hi = v.astype(BF16).astype(F32)
    mid = (v - hi).astype(BF16).astype(F32)
    return jnp.concatenate([hi, mid, v - hi - mid, jnp.zeros_like(v)], axis=0).astype(BF16)


def parent(j):
    return max(r for r in (0,) + RELAYS if r < j)


def iota(shape, dim):
    return lax.broadcasted_iota(jnp.int32, shape, dim)


def kernel(
    x_hbm, z_hbm, b_hbm, c_hbm, dt_hbm, ld_hbm, skip_hbm, gain_hbm, w_ref,
    out_ref,
    x_ref, z_ref, b_ref, c_ref, dt_ref, ld_ref, skip_ref, gain_ref,
    wbuf, drow, dsib, lown, lsib, pbuf, recva, retbuf, inbuf, insib, hid, ssq, sendb, recvb, acc, o2, osend,
    ylocal, gsil, expx_s,
    ins, wl_sem, ws, wr, as_, ar, bs, br, ds, dr, rs_s, rs_r,
):
    s = lax.axis_index("seq")
    h = lax.axis_index("head")
    k = s // 2
    c = lax.rem(s, 2)
    cx = k // NY
    cy = lax.rem(k, NY)
    sib = (k * 2 + 1 - c, h)

    def chip(a, b):
        return lax.rem(cx + a, NY) * NY + lax.rem(cy + b, NY)

    offs = [(a, b) for a in range(NY) for b in range(NY) if (a, b) != (0, 0)]
    offs.sort(key=lambda o: -(min(o[0], NY - o[0]) + min(o[1], NY - o[1])))
    hops = sorted({j - parent(j) for j in range(1, NZ // 2 + 1)})
    zs = [d for a in hops for d in (a, NZ - a)]

    loads = []
    for n, (src, dst) in enumerate((
        (ld_hbm, ld_ref), (dt_hbm, dt_ref), (x_hbm, x_ref), (b_hbm, b_ref), (c_hbm, c_ref),
        (skip_hbm, skip_ref), (z_hbm, z_ref), (gain_hbm, gain_ref),
    )):
        cp = pltpu.make_async_copy(src, dst, ins.at[n])
        cp.start()
        loads.append(cp)

    partners = [sib]
    partners += [(chip(a, b) * 2 + c, h) for a, b in offs]
    partners += [(s, lax.rem(h + d, NZ)) for d in zs]
    barrier = pltpu.get_barrier_semaphore()
    for p in partners:
        pl.semaphore_signal(barrier, inc=1, device_id=p, device_id_type=MESH)
    wl = pltpu.make_async_copy(w_ref, wbuf.at[k], wl_sem)
    wl.start()

    row = iota((128, 128), 0)
    col = iota((128, 128), 1)
    eye = (row == col).astype(F32)
    lower = row >= col
    loads[0].wait()
    loads[1].wait()
    ld = ld_ref[...]
    dt = dt_ref[...]
    sums3 = nt(split3(ld), lower.astype(BF16))
    run_r = sums3[0:8] + sums3[8:16] + sums3[16:24]
    heads = (iota((8, 512), 1) // 64 == iota((8, 512), 0)).astype(F32)
    heads4 = (iota((32, 512), 1) // 64 == lax.rem(iota((32, 512), 0), 8)).astype(BF16)

    def expand(v):
        return lax.dot_general(
            split3(v), heads4, (((0,), (0,)), ((), ())), preferred_element_type=F32
        )

    total_h = run_r[:, 127:128]
    total = jnp.sum(total_h * heads, axis=0, keepdims=True)
    drow[...] = jnp.broadcast_to(total, (8, 512))

    def to_sib(src, dst, n):
        return pltpu.make_async_remote_copy(
            src_ref=src, dst_ref=dst, send_sem=ds.at[n], recv_sem=dr.at[n],
            device_id=sib, device_id_type=MESH,
        )

    tailx = expand(jnp.exp(total_h - run_r) * dt)
    loads[2].wait()
    xf = x_ref[...].astype(F32)
    xt = (xf * tailx).astype(BF16)
    loads[3].wait()
    keys = b_ref[...]
    state = lax.dot_general(keys, xt, (((0,), (0,)), ((), ())), preferred_element_type=F32)
    lown[...] = state.astype(BF16)
    pl.semaphore_wait(barrier, len(partners))

    swap = to_sib(drow, dsib, 0)
    swap.start()

    w_sent = []

    def w_copy(src, kk, half, dx, dy, dest):
        return pltpu.make_async_remote_copy(
            src_ref=src, dst_ref=wbuf.at[kk, pl.ds(256 * half, 256)],
            send_sem=ws.at[len(w_sent)], recv_sem=wr.at[half, NY * dx + dy],
            device_id=(dest * 2 + c, h), device_id_type=MESH,
        )

    def send_w(src, kk, half, dx, dy, dest):
        cp = w_copy(src, kk, half, dx, dy, dest)
        cp.start()
        w_sent.append(cp)

    def own_w(half):
        return w_ref.at[pl.ds(256 * half, 256)]

    def wait_w(half, kk, at):
        pltpu.make_async_remote_copy(
            src_ref=wbuf.at[kk, pl.ds(256 * half, 256)], dst_ref=wbuf.at[kk, pl.ds(256 * half, 256)],
            send_sem=ws.at[0], recv_sem=wr.at[half, at], device_id=sib, device_id_type=MESH,
        ).wait_recv()

    def pass_on(which):
        for d, half in which:
            if half == 0:
                kk = chip(0, NY - d)
                wait_w(0, kk, NY - d)
                for e in (2, 1, 3):
                    send_w(wbuf.at[kk, pl.ds(0, 256)], kk, 0, NY - e, NY - d, chip(e, 0))
            else:
                kk = chip(NY - d, 0)
                wait_w(1, kk, NY * (NY - d))
                for e in (2, 1, 3):
                    send_w(wbuf.at[kk, pl.ds(256, 256)], kk, 1, NY - d, NY - e, chip(0, e))

    for d in (2, 1, 3):
        send_w(own_w(0), k, 0, 0, NY - d, chip(0, d))
        send_w(own_w(1), k, 1, NY - d, 0, chip(d, 0))

    swap.wait()
    first_core = jnp.full((1, 1), c, jnp.int32) == 0
    d_sib = dsib[0:1, :]
    decay_p = total + d_sib
    pair = (state * jnp.where(first_core, jnp.exp(d_sib), 1.0)).astype(BF16)
    hi = decay_p.astype(BF16).astype(F32)
    mid = (decay_p - hi).astype(BF16).astype(F32)
    low = decay_p - hi - mid
    r16 = iota((16, 512), 0)
    parts = jnp.where(r16 == 0, hi, jnp.where(r16 == 1, mid, jnp.where(r16 == 2, low, 0.0)))
    parts = parts.astype(BF16)
    for q in range(NCHIP):
        n0, l0 = 32 * (q % 4), 128 * (q // 4)
        pbuf[q, 0:32, :] = pair[n0 : n0 + 32, l0 : l0 + 128]
        pbuf[q, 32:48, :] = parts[:, l0 : l0 + 128]
    to_owner = []
    for n, (a, b) in enumerate(offs):
        q = chip(a, b)
        cp = pltpu.make_async_remote_copy(
            src_ref=pbuf.at[q], dst_ref=recva.at[k], send_sem=as_.at[n], recv_sem=ar.at[n],
            device_id=(q * 2 + c, h), device_id_type=MESH,
        )
        cp.start()
        to_owner.append(cp)
    recva[k] = pbuf[k]
    swap1 = to_sib(lown, lsib, 1)
    swap1.start()
    for d in (2, 1, 3):
        send_w(own_w(0), k, 0, NY - d, 0, chip(d, 0))
        send_w(own_w(1), k, 1, 0, NY - d, chip(0, d))

    for cp in loads[4:]:
        cp.wait()
    queries = c_ref[...]
    skip = jnp.dot(skip_ref[...], heads, precision=HIGH, preferred_element_type=F32)
    scores = nt(queries, keys)
    lane = iota((128, 128), 1)
    run_c = nt(lower.astype(F32), ld, HIGH)
    expx_s[...] = expand(jnp.exp(run_r))
    for p in range(4):
        xp = x_ref[:, 128 * p : 128 * p + 128]
        ys = []
        for hh in (2 * p, 2 * p + 1):
            spread = run_c[:, hh : hh + 1] - run_r[hh : hh + 1, :]
            m = jnp.exp(jnp.where(lower, spread, -1e30)) * (scores * dt[hh : hh + 1, :])
            ys.append(jnp.dot(m.astype(BF16), xp, preferred_element_type=F32))
        ylocal[:, 128 * p : 128 * p + 128] = (
            jnp.where(lane < 64, ys[0], ys[1])
            + skip[:, 128 * p : 128 * p + 128] * xp.astype(F32)
        )
    zf = z_ref[...].astype(F32)
    gsil[...] = zf / (1.0 + jnp.exp(-zf))
    swap1.wait()
    other = jnp.dot(queries, lsib[...], preferred_element_type=F32)
    early_x = jnp.where(first_core, 1.0, jnp.exp(d_sib))
    ylocal[...] = ylocal[...] + expx_s[...] * jnp.where(first_core, 0.0, other)
    expx_s[...] = expx_s[...] * early_x

    for cp in to_owner:
        cp.wait_recv()
    carry = jnp.zeros((32, 128), F32)
    for kk in range(NCHIP):
        retbuf[kk] = carry.astype(BF16)
        m = recva[kk].astype(F32)
        carry = jnp.exp(m[32:33] + m[33:34] + m[34:35]) * carry + m[0:32]
    back = []
    for n, (a, b) in enumerate(offs):
        q = chip(a, b)
        cp = pltpu.make_async_remote_copy(
            src_ref=retbuf.at[q], dst_ref=inbuf.at[k], send_sem=bs.at[n], recv_sem=br.at[n],
            device_id=(q * 2 + c, h), device_id_type=MESH,
        )
        cp.start()
        back.append(cp)
    inbuf[k] = retbuf[k]
    pass_on(PASSED)
    wl.wait()

    for cp in back:
        cp.wait_recv()
    swap2 = to_sib(inbuf, insib, 4)
    swap2.start()

    def carried(ref, p):
        part = ref[4 * p : 4 * p + 4].reshape(128, 128)
        return jnp.dot(queries, part, preferred_element_type=F32)

    for p in range(4):
        l0 = 128 * p
        ylocal[:, l0 : l0 + 128] = ylocal[:, l0 : l0 + 128] + (
            carried(inbuf, p) * expx_s[:, l0 : l0 + 128]
        )
    swap2.wait()

    squares = jnp.zeros((8, 128), F32)
    gain = gain_ref[...]
    for p in range(4):
        l0 = 128 * p
        y = ylocal[:, l0 : l0 + 128] + carried(insib, p) * expx_s[:, l0 : l0 + 128]
        g = y * gsil[:, l0 : l0 + 128]
        squares = squares + nt(jnp.ones((8, 128), F32), g * g, HIGH)
        hid[c, :, l0 : l0 + 128] = (g * gain[:, l0 : l0 + 128]).astype(BF16)
    ssq[c] = squares
    swap3 = to_sib(hid.at[c], hid.at[c], 2)
    swap3.start()
    swap4 = to_sib(ssq.at[c], ssq.at[c], 3)
    swap4.start()
    swap3.wait()
    swap4.wait()

    sides = {0: 8, 1: 7}
    slot = {}
    for side, most in sides.items():
        for j in range(1, most + 1):
            slot[side, j] = len(slot)
    halves = (1 - c, c)
    own_sq = [ssq[t, 0:1, :] for t in halves]
    r16 = iota((16, 128), 0)

    def target(side, j):
        return lax.rem(h + (NZ - j if side == 0 else j), NZ)

    def split_sq(sq):
        ext = jnp.zeros((16, 128), F32)
        for t, v in enumerate(sq):
            top = v.astype(BF16).astype(F32)
            ext = jnp.where(r16 == 2 * t, top, jnp.where(r16 == 2 * t + 1, v - top, ext))
        return ext.astype(BF16)

    own_ext = split_sq(own_sq)
    sent = {}

    def send(side, j, t):
        n = slot[side, j]
        rows = pl.ds(0, 128 if t else 144)
        cp = pltpu.make_async_remote_copy(
            src_ref=sendb.at[n, t, rows], dst_ref=recvb.at[n, t, rows],
            send_sem=rs_s.at[n, t], recv_sem=rs_r.at[n, t],
            device_id=(s, target(side, j - parent(j))), device_id_type=MESH,
        )
        cp.start()
        sent[side, j, t] = cp

    def project(dest):
        at = lax.rem(dest // NY - cx + NY, NY) * NY + lax.rem(lax.rem(dest, NY) - cy + NY, NY)

        for half in (0, 1):
            @pl.when(at >= NY if half == 0 else lax.rem(at, NY) > 0)
            def _(half=half):
                wait_w(half, dest, at)

        wb = wbuf[dest]
        return [jnp.dot(hid[t], wb, preferred_element_type=F32) for t in halves]

    def leaf(side, j):
        n = slot[side, j]
        for t, part in enumerate(project(target(side, j))):
            sendb[n, t, 0:128, :] = part.astype(BF16)
        sendb[n, 0, 128:144, :] = own_ext

    def prepare(n, dest):
        for t, part in enumerate(project(dest)):
            acc[n, t] = part

    def gather(n, t, kids):
        part = acc[n, t]
        sq = list(own_sq)
        for side, i in kids:
            sent[side, i, t].wait_recv()
            got = recvb[slot[side, i], t].astype(F32)
            part = part + got[0:128]
            for u in (0, 1):
                sq[u] = sq[u] + got[128 + 2 * u : 129 + 2 * u] + got[129 + 2 * u : 130 + 2 * u]
        return part, sq

    def relay(side, j, t):
        kids = [(side, i) for i in range(j + 1, sides[side] + 1) if parent(i) == j]
        part, sq = gather(RELAYS.index(j) * 2 + side, t, kids)
        n = slot[side, j]
        sendb[n, t, 0:128, :] = part.astype(BF16)
        if t == 0:
            sendb[n, 0, 128:144, :] = split_sq(sq)
        send(side, j, t)

    both = (0, 1)
    for step in ORDER:
        kind, j, t = step[0], int(step[1]), int(step[2:] or 0)
        if j == 0:
            prepare(2 * len(RELAYS), h)
            continue
        for side in both:
            if (side, j) not in slot:
                continue
            if kind == "P":
                prepare(RELAYS.index(j) * 2 + side, target(side, j))
            elif kind == "R":
                relay(side, j, t)
            else:
                if kind in "LX":
                    leaf(side, j)
                if kind in "SX":
                    send(side, j, t)

    last = [(side, i) for side in both for i in range(1, 9) if (side, i) in slot and parent(i) == 0]
    for t in (0, 1):
        part, sq = gather(2 * len(RELAYS), t, last)
        if t == 0:
            scale = [lax.rsqrt(v * (1.0 / 8192.0) + 1e-05) for v in sq]
            scale = [jnp.broadcast_to(v, (8, 128)).T[:, 0:1] for v in scale]
        done = (part * scale[t]).astype(BF16)
        if t == 0:
            osend[...] = done
            swap5 = to_sib(osend, o2.at[c], 5)
            swap5.start()
        else:
            o2[c] = done
    for cp in w_sent + to_owner + back + list(sent.values()):
        cp.wait_send()
    swap5.wait()
    out_ref[:, 0:128] = o2[0]
    out_ref[:, 128:256] = o2[1]


def body(
    signal, gate_input, state_in, state_out, step_size, log_decay, skip_gain, norm_gain, out_weight
):
    vmem = pl.BlockSpec(memory_space=pltpu.VMEM)
    args = [pltpu.with_memory_space_constraint(a, pltpu.HBM) for a in (
        signal, gate_input, state_in, state_out, step_size, log_decay,
        skip_gain.reshape(1, -1), norm_gain.reshape(1, -1), out_weight,
    )]
    dma = pltpu.SemaphoreType.DMA
    return pl.pallas_call(
        kernel,
        out_shape=jax.ShapeDtypeStruct((128, 256), BF16),
        in_specs=[pl.BlockSpec(memory_space=pltpu.HBM)] * 9,
        out_specs=vmem,
        scratch_shapes=[
            pltpu.VMEM((128, 512), BF16),
            pltpu.VMEM((128, 512), BF16),
            pltpu.VMEM((128, 128), BF16),
            pltpu.VMEM((128, 128), BF16),
            pltpu.VMEM((8, 128), F32),
            pltpu.VMEM((8, 128), F32),
            pltpu.VMEM((1, 8), F32),
            pltpu.VMEM((1, 512), F32),
            pltpu.VMEM((NCHIP, 512, 128), BF16),
            pltpu.VMEM((8, 512), F32),
            pltpu.VMEM((8, 512), F32),
            pltpu.VMEM((128, 512), BF16),
            pltpu.VMEM((128, 512), BF16),
            pltpu.VMEM((NCHIP, 48, 128), BF16),
            pltpu.VMEM((NCHIP, 48, 128), BF16),
            pltpu.VMEM((NCHIP, 32, 128), BF16),
            pltpu.VMEM((NCHIP, 32, 128), BF16),
            pltpu.VMEM((NCHIP, 32, 128), BF16),
            pltpu.VMEM((2, 128, 512), BF16),
            pltpu.VMEM((2, 8, 128), F32),
            pltpu.VMEM((15, 2, 144, 128), BF16),
            pltpu.VMEM((15, 2, 144, 128), BF16),
            pltpu.VMEM((7, 2, 128, 128), F32),
            pltpu.VMEM((2, 128, 128), BF16),
            pltpu.VMEM((128, 128), BF16),
            pltpu.VMEM((128, 512), F32),
            pltpu.VMEM((128, 512), F32),
            pltpu.VMEM((128, 512), F32),
            dma((8,)),
            dma,
            dma((30,)), dma((2, 16)),
            dma((15,)), dma((15,)),
            dma((15,)), dma((15,)),
            dma((6,)), dma((6,)),
            dma((15, 2)), dma((15, 2)),
        ],
        compiler_params=pltpu.CompilerParams(
            collective_id=0, has_side_effects=True, vmem_limit_bytes=40 * 2**20
        ),
        name="ssd_layer",
    )(*args)


def solution(mesh):
    in_specs = (
        P("seq", "head"),
        P("seq", "head"),
        P("seq", None),
        P("seq", None),
        P("head", "seq"),
        P("head", "seq"),
        P("head"),
        P("head"),
        P("head", "seq"),
    )
    out_specs = P("seq", "head")
    return jax.shard_map(body, mesh=mesh, in_specs=in_specs, out_specs=out_specs, check_vma=False)
```

```python
import jax
import jax.numpy as jnp
from jax import lax
from jax.experimental import pallas as pl
from jax.experimental.pallas import tpu as pltpu
from jax.sharding import PartitionSpec as P

MESH = pl.DeviceIdType.MESH
HIGH = lax.Precision.HIGHEST
F32 = jnp.float32
BF16 = jnp.bfloat16
NY = 4
NCHIP = 16
PASSED = ((2, 0), (2, 1), (1, 0), (1, 1), (3, 0), (3, 1))
NZ = 16
RELAYS = (2, 4, 6)
ORDER = (
    "X8", "X7", "S81", "S71", "X5", "P6", "R60", "S51",
    "R61", "X3", "P4", "R40", "S31", "R41", "X1", "P2",
    "R20", "S11", "R21", "P0",
)


def nt(a, b, precision=None):
    return lax.dot_general(
        a, b, (((1,), (1,)), ((), ())), precision=precision, preferred_element_type=F32
    )


def split3(v):
    hi = v.astype(BF16).astype(F32)
    mid = (v - hi).astype(BF16).astype(F32)
    return jnp.concatenate([hi, mid, v - hi - mid, jnp.zeros_like(v)], axis=0).astype(BF16)


def parent(j):
    return max(r for r in (0,) + RELAYS if r < j)


def iota(shape, dim):
    return lax.broadcasted_iota(jnp.int32, shape, dim)


def kernel(
    x_hbm, z_hbm, b_hbm, c_hbm, dt_hbm, ld_hbm, skip_hbm, gain_hbm, w_ref,
    out_ref,
    x_ref, z_ref, b_ref, c_ref, dt_ref, ld_ref, skip_ref, gain_ref,
    wbuf, sbuf, lbuf, pbuf, recva, retbuf, inbuf, incs, incall, hid, ssq, sendb, recvb, acc, o2, osend,
    ylocal, gsil, expx_s,
    ins, wl_sem, ws, wr, as_, ar, bs, br, ds, dr, rs_s, rs_r,
):
    s = lax.axis_index("seq")
    h = lax.axis_index("head")
    k = s // 2
    c = lax.rem(s, 2)
    cx = k // NY
    cy = lax.rem(k, NY)
    sib = (k * 2 + 1 - c, h)

    def chip(a, b):
        return lax.rem(cx + a, NY) * NY + lax.rem(cy + b, NY)

    offs = [(a, b) for a in range(NY) for b in range(NY) if (a, b) != (0, 0)]
    offs.sort(key=lambda o: -(min(o[0], NY - o[0]) + min(o[1], NY - o[1])))
    hops = sorted({j - parent(j) for j in range(1, NZ // 2 + 1)})
    zs = [d for a in hops for d in (a, NZ - a)]

    loads = []
    for n, (src, dst) in enumerate((
        (ld_hbm, ld_ref), (dt_hbm, dt_ref), (x_hbm, x_ref), (b_hbm, b_ref), (c_hbm, c_ref),
        (skip_hbm, skip_ref), (z_hbm, z_ref), (gain_hbm, gain_ref),
    )):
        cp = pltpu.make_async_copy(src, dst, ins.at[n])
        cp.start()
        loads.append(cp)

    partners = [sib]
    partners += [(chip(a, b) * 2 + c, h) for a, b in offs]
    partners += [(s, lax.rem(h + d, NZ)) for d in zs]
    barrier = pltpu.get_barrier_semaphore()
    for p in partners:
        pl.semaphore_signal(barrier, inc=1, device_id=p, device_id_type=MESH)
    wl = pltpu.make_async_copy(w_ref, wbuf.at[k], wl_sem)
    wl.start()

    row = iota((128, 128), 0)
    col = iota((128, 128), 1)
    eye = (row == col).astype(F32)
    lower = row >= col
    loads[0].wait()
    loads[1].wait()
    ld = ld_ref[...]
    dt = dt_ref[...]
    sums3 = nt(split3(ld), lower.astype(BF16))
    run_r = sums3[0:8] + sums3[8:16] + sums3[16:24]
    heads = (iota((8, 512), 1) // 64 == iota((8, 512), 0)).astype(F32)
    heads4 = (iota((32, 512), 1) // 64 == lax.rem(iota((32, 512), 0), 8)).astype(BF16)

    def expand(v):
        return lax.dot_general(
            split3(v), heads4, (((0,), (0,)), ((), ())), preferred_element_type=F32
        )

    total_h = run_r[:, 127:128]
    tailx = expand(jnp.exp(total_h - run_r) * dt)
    total = jnp.sum(total_h * heads, axis=0, keepdims=True)
    loads[2].wait()
    xf = x_ref[...].astype(F32)
    xt = (xf * tailx).astype(BF16)
    loads[3].wait()
    keys = b_ref[...]
    state = lax.dot_general(keys, xt, (((0,), (0,)), ((), ())), preferred_element_type=F32)
    for hf in range(2):
        sbuf[hf, 0:128, :] = state[:, 256 * hf : 256 * hf + 256]
        sbuf[hf, 128:136, :] = jnp.broadcast_to(total[:, 256 * hf : 256 * hf + 256], (8, 256))

    pl.semaphore_wait(barrier, len(partners))

    def to_sib(src, dst, n):
        return pltpu.make_async_remote_copy(
            src_ref=src, dst_ref=dst, send_sem=ds.at[n], recv_sem=dr.at[n],
            device_id=sib, device_id_type=MESH,
        )

    swap = to_sib(sbuf.at[1 - c], lbuf, 0)
    swap.start()

    w_sent = []

    def w_copy(src, kk, half, dx, dy, dest):
        return pltpu.make_async_remote_copy(
            src_ref=src, dst_ref=wbuf.at[kk, pl.ds(256 * half, 256)],
            send_sem=ws.at[len(w_sent)], recv_sem=wr.at[half, NY * dx + dy],
            device_id=(dest * 2 + c, h), device_id_type=MESH,
        )

    def send_w(src, kk, half, dx, dy, dest):
        cp = w_copy(src, kk, half, dx, dy, dest)
        cp.start()
        w_sent.append(cp)

    def own_w(half):
        return w_ref.at[pl.ds(256 * half, 256)]

    def wait_w(half, kk, at):
        pltpu.make_async_remote_copy(
            src_ref=wbuf.at[kk, pl.ds(256 * half, 256)], dst_ref=wbuf.at[kk, pl.ds(256 * half, 256)],
            send_sem=ws.at[0], recv_sem=wr.at[half, at], device_id=sib, device_id_type=MESH,
        ).wait_recv()

    def pass_on(which):
        for d, half in which:
            if half == 0:
                kk = chip(0, NY - d)
                wait_w(0, kk, NY - d)
                for e in (2, 1, 3):
                    send_w(wbuf.at[kk, pl.ds(0, 256)], kk, 0, NY - e, NY - d, chip(e, 0))
            else:
                kk = chip(NY - d, 0)
                wait_w(1, kk, NY * (NY - d))
                for e in (2, 1, 3):
                    send_w(wbuf.at[kk, pl.ds(256, 256)], kk, 1, NY - d, NY - e, chip(0, e))

    for d in (2, 1, 3):
        send_w(own_w(0), k, 0, 0, NY - d, chip(0, d))
        send_w(own_w(1), k, 1, NY - d, 0, chip(d, 0))

    swap.wait()
    mine = sbuf[c]
    other = lbuf[...]
    early_own = jnp.full((1, 1), c, jnp.int32) == 0
    early = jnp.where(early_own, mine, other)
    later = jnp.where(early_own, other, mine)
    state_e = early[0:128]
    decay_e = early[128:129]
    decay_o = later[128:129]
    pair = (jnp.exp(decay_o) * state_e + later[0:128]).astype(BF16)
    decay_p = decay_e + decay_o
    hi = decay_p.astype(BF16).astype(F32)
    mid = (decay_p - hi).astype(BF16).astype(F32)
    low = decay_p - hi - mid
    r16 = iota((16, 256), 0)
    parts = jnp.where(r16 == 0, hi, jnp.where(r16 == 1, mid, jnp.where(r16 == 2, low, 0.0)))
    parts = parts.astype(BF16)
    for q in range(NCHIP):
        n0, l0 = 16 * (q % 8), 128 * (q // 8)
        pbuf[q, 0:16, :] = pair[n0 : n0 + 16, l0 : l0 + 128]
        pbuf[q, 16:32, :] = parts[:, l0 : l0 + 128]
    to_owner = []
    for n, (a, b) in enumerate(offs):
        q = chip(a, b)
        cp = pltpu.make_async_remote_copy(
            src_ref=pbuf.at[q, pl.ds(0, 24)], dst_ref=recva.at[k, pl.ds(0, 24)], send_sem=as_.at[n], recv_sem=ar.at[n],
            device_id=(q * 2 + c, h), device_id_type=MESH,
        )
        cp.start()
        to_owner.append(cp)
    recva[k, 0:24] = pbuf[k, 0:24]
    for d in (2, 1, 3):
        send_w(own_w(0), k, 0, NY - d, 0, chip(d, 0))
        send_w(own_w(1), k, 1, 0, NY - d, chip(0, d))

    for cp in loads[4:]:
        cp.wait()
    queries = c_ref[...]
    skip = jnp.dot(skip_ref[...], heads, precision=HIGH, preferred_element_type=F32)
    scores = nt(queries, keys)
    lane = iota((128, 128), 1)
    run_c = nt(lower.astype(F32), ld, HIGH)
    expx_s[...] = expand(jnp.exp(run_r))
    for p in range(4):
        xp = x_ref[:, 128 * p : 128 * p + 128]
        ys = []
        for hh in (2 * p, 2 * p + 1):
            spread = run_c[:, hh : hh + 1] - run_r[hh : hh + 1, :]
            m = jnp.exp(jnp.where(lower, spread, -1e30)) * (scores * dt[hh : hh + 1, :])
            ys.append(jnp.dot(m.astype(BF16), xp, preferred_element_type=F32))
        ylocal[:, 128 * p : 128 * p + 128] = (
            jnp.where(lane < 64, ys[0], ys[1])
            + skip[:, 128 * p : 128 * p + 128] * xp.astype(F32)
        )
    zf = z_ref[...].astype(F32)
    gsil[...] = zf / (1.0 + jnp.exp(-zf))

    for cp in to_owner:
        cp.wait_recv()
    carry = jnp.zeros((16, 128), F32)
    for kk in range(NCHIP):
        retbuf[kk] = carry.astype(BF16)
        m = recva[kk, 0:24].astype(F32)
        carry = jnp.exp(m[16:17] + m[17:18] + m[18:19]) * carry + m[0:16]
    back = []
    for n, (a, b) in enumerate(offs):
        q = chip(a, b)
        cp = pltpu.make_async_remote_copy(
            src_ref=retbuf.at[q], dst_ref=inbuf.at[k], send_sem=bs.at[n], recv_sem=br.at[n],
            device_id=(q * 2 + c, h), device_id_type=MESH,
        )
        cp.start()
        back.append(cp)
    inbuf[k] = retbuf[k]
    pass_on(PASSED)
    wl.wait()

    for cp in back:
        cp.wait_recv()
    incoming = jnp.concatenate(
        [inbuf[8 * i : 8 * i + 8].reshape(128, 128).astype(F32) for i in range(2)], axis=1
    )
    inc_odd = jnp.exp(decay_e) * incoming + state_e
    incs[...] = jnp.where(early_own, inc_odd, incoming).astype(BF16)
    swap2 = to_sib(incs, incall.at[c], 1)
    swap2.start()
    incall[c] = jnp.where(early_own, incoming, inc_odd).astype(BF16)
    swap2.wait()

    gain = gain_ref[...]
    for hf in range(2):
        l0 = 256 * hf
        carried = jnp.dot(queries, incall[hf], preferred_element_type=F32)
        y = ylocal[:, l0 : l0 + 256] + carried * expx_s[:, l0 : l0 + 256]
        g = y * gsil[:, l0 : l0 + 256]
        square = g * g if hf == 0 else square + g * g
        hid[c, :, l0 : l0 + 256] = (g * gain[:, l0 : l0 + 256]).astype(BF16)
    swap3 = to_sib(hid.at[c], hid.at[c], 2)
    swap3.start()
    ssq[c] = nt(jnp.ones((8, 256), F32), square, HIGH)
    swap4 = to_sib(ssq.at[c], ssq.at[c], 3)
    swap4.start()
    swap3.wait()
    swap4.wait()

    sides = {0: 8, 1: 7}
    slot = {}
    for side, most in sides.items():
        for j in range(1, most + 1):
            slot[side, j] = len(slot)
    halves = (1 - c, c)
    own_sq = [ssq[t, 0:1, :] for t in halves]
    r16 = iota((16, 128), 0)

    def target(side, j):
        return lax.rem(h + (NZ - j if side == 0 else j), NZ)

    def split_sq(sq):
        ext = jnp.zeros((16, 128), F32)
        for t, v in enumerate(sq):
            top = v.astype(BF16).astype(F32)
            ext = jnp.where(r16 == 2 * t, top, jnp.where(r16 == 2 * t + 1, v - top, ext))
        return ext.astype(BF16)

    own_ext = split_sq(own_sq)
    sent = {}

    def send(side, j, t):
        n = slot[side, j]
        rows = pl.ds(0, 128 if t else 144)
        cp = pltpu.make_async_remote_copy(
            src_ref=sendb.at[n, t, rows], dst_ref=recvb.at[n, t, rows],
            send_sem=rs_s.at[n, t], recv_sem=rs_r.at[n, t],
            device_id=(s, target(side, j - parent(j))), device_id_type=MESH,
        )
        cp.start()
        sent[side, j, t] = cp

    def project(dest):
        at = lax.rem(dest // NY - cx + NY, NY) * NY + lax.rem(lax.rem(dest, NY) - cy + NY, NY)

        for half in (0, 1):
            @pl.when(at >= NY if half == 0 else lax.rem(at, NY) > 0)
            def _(half=half):
                wait_w(half, dest, at)

        wb = wbuf[dest]
        return [jnp.dot(hid[t], wb, preferred_element_type=F32) for t in halves]

    def leaf(side, j):
        n = slot[side, j]
        for t, part in enumerate(project(target(side, j))):
            sendb[n, t, 0:128, :] = part.astype(BF16)
        sendb[n, 0, 128:144, :] = own_ext

    def prepare(n, dest):
        for t, part in enumerate(project(dest)):
            acc[n, t] = part

    def gather(n, t, kids):
        part = acc[n, t]
        sq = list(own_sq)
        for side, i in kids:
            sent[side, i, t].wait_recv()
            got = recvb[slot[side, i], t].astype(F32)
            part = part + got[0:128]
            for u in (0, 1):
                sq[u] = sq[u] + got[128 + 2 * u : 129 + 2 * u] + got[129 + 2 * u : 130 + 2 * u]
        return part, sq

    def relay(side, j, t):
        kids = [(side, i) for i in range(j + 1, sides[side] + 1) if parent(i) == j]
        part, sq = gather(RELAYS.index(j) * 2 + side, t, kids)
        n = slot[side, j]
        sendb[n, t, 0:128, :] = part.astype(BF16)
        if t == 0:
            sendb[n, 0, 128:144, :] = split_sq(sq)
        send(side, j, t)

    both = (0, 1)
    for step in ORDER:
        kind, j, t = step[0], int(step[1]), int(step[2:] or 0)
        if j == 0:
            prepare(2 * len(RELAYS), h)
            continue
        for side in both:
            if (side, j) not in slot:
                continue
            if kind == "P":
                prepare(RELAYS.index(j) * 2 + side, target(side, j))
            elif kind == "R":
                relay(side, j, t)
            else:
                if kind in "LX":
                    leaf(side, j)
                if kind in "SX":
                    send(side, j, t)

    last = [(side, i) for side in both for i in range(1, 9) if (side, i) in slot and parent(i) == 0]
    for t in (0, 1):
        part, sq = gather(2 * len(RELAYS), t, last)
        if t == 0:
            scale = [lax.rsqrt(v * (1.0 / 8192.0) + 1e-05) for v in sq]
            scale = [jnp.broadcast_to(v, (8, 128)).T[:, 0:1] for v in scale]
        done = (part * scale[t]).astype(BF16)
        if t == 0:
            osend[...] = done
            swap5 = to_sib(osend, o2.at[c], 4)
            swap5.start()
        else:
            o2[c] = done
    for cp in w_sent + to_owner + back + list(sent.values()):
        cp.wait_send()
    swap5.wait()
    out_ref[:, 0:128] = o2[0]
    out_ref[:, 128:256] = o2[1]


def body(
    signal, gate_input, state_in, state_out, step_size, log_decay, skip_gain, norm_gain, out_weight
):
    vmem = pl.BlockSpec(memory_space=pltpu.VMEM)
    args = [pltpu.with_memory_space_constraint(a, pltpu.HBM) for a in (
        signal, gate_input, state_in, state_out, step_size, log_decay,
        skip_gain.reshape(1, -1), norm_gain.reshape(1, -1), out_weight,
    )]
    dma = pltpu.SemaphoreType.DMA
    return pl.pallas_call(
        kernel,
        out_shape=jax.ShapeDtypeStruct((128, 256), BF16),
        in_specs=[pl.BlockSpec(memory_space=pltpu.HBM)] * 9,
        out_specs=vmem,
        scratch_shapes=[
            pltpu.VMEM((128, 512), BF16),
            pltpu.VMEM((128, 512), BF16),
            pltpu.VMEM((128, 128), BF16),
            pltpu.VMEM((128, 128), BF16),
            pltpu.VMEM((8, 128), F32),
            pltpu.VMEM((8, 128), F32),
            pltpu.VMEM((1, 8), F32),
            pltpu.VMEM((1, 512), F32),
            pltpu.VMEM((NCHIP, 512, 128), BF16),
            pltpu.VMEM((2, 136, 256), F32),
            pltpu.VMEM((136, 256), F32),
            pltpu.VMEM((NCHIP, 32, 128), BF16),
            pltpu.VMEM((NCHIP, 32, 128), BF16),
            pltpu.VMEM((NCHIP, 16, 128), BF16),
            pltpu.VMEM((NCHIP, 16, 128), BF16),
            pltpu.VMEM((128, 256), BF16),
            pltpu.VMEM((2, 128, 256), BF16),
            pltpu.VMEM((2, 128, 512), BF16),
            pltpu.VMEM((2, 8, 128), F32),
            pltpu.VMEM((15, 2, 144, 128), BF16),
            pltpu.VMEM((15, 2, 144, 128), BF16),
            pltpu.VMEM((7, 2, 128, 128), F32),
            pltpu.VMEM((2, 128, 128), BF16),
            pltpu.VMEM((128, 128), BF16),
            pltpu.VMEM((128, 512), F32),
            pltpu.VMEM((128, 512), F32),
            pltpu.VMEM((128, 512), F32),
            dma((8,)),
            dma,
            dma((30,)), dma((2, 16)),
            dma((15,)), dma((15,)),
            dma((15,)), dma((15,)),
            dma((5,)), dma((5,)),
            dma((15, 2)), dma((15, 2)),
        ],
        compiler_params=pltpu.CompilerParams(
            collective_id=0, has_side_effects=True, vmem_limit_bytes=40 * 2**20
        ),
        name="ssd_layer",
    )(*args)


def solution(mesh):
    in_specs = (
        P("seq", "head"),
        P("seq", "head"),
        P("seq", None),
        P("seq", None),
        P("head", "seq"),
        P("head", "seq"),
        P("head"),
        P("head"),
        P("head", "seq"),
    )
    out_specs = P("seq", "head")
    return jax.shard_map(body, mesh=mesh, in_specs=in_specs, out_specs=out_specs, check_vma=False)
```

```python
import jax
import jax.numpy as jnp
from jax import lax
from jax.experimental import pallas as pl
from jax.experimental.pallas import tpu as pltpu
from jax.sharding import PartitionSpec as P

MESH = pl.DeviceIdType.MESH
HIGH = lax.Precision.HIGHEST
F32 = jnp.float32
BF16 = jnp.bfloat16
NY = 4
NCHIP = 16
PASSED = ((1, 0), (1, 1), (3, 0), (3, 1), (2, 0), (2, 1))
NZ = 16
RELAYS = (2, 4, 6)
ORDER = (
    "X8", "X7", "S81", "S71", "X5", "P6", "R60", "S51",
    "R61", "X3", "P4", "R40", "S31", "R41", "X1", "P2",
    "R20", "S11", "R21", "P0",
)


def nt(a, b, precision=None):
    return lax.dot_general(
        a, b, (((1,), (1,)), ((), ())), precision=precision, preferred_element_type=F32
    )


def split3(v):
    hi = v.astype(BF16).astype(F32)
    mid = (v - hi).astype(BF16).astype(F32)
    return jnp.concatenate([hi, mid, v - hi - mid, jnp.zeros_like(v)], axis=0).astype(BF16)


def parent(j):
    return max(r for r in (0,) + RELAYS if r < j)


def iota(shape, dim):
    return lax.broadcasted_iota(jnp.int32, shape, dim)


def kernel(
    x_hbm, z_hbm, b_hbm, c_hbm, dt_hbm, ld_hbm, skip_hbm, gain_hbm, w_ref,
    out_ref,
    x_ref, z_ref, b_ref, c_ref, dt_ref, ld_ref, skip_ref, gain_ref,
    wbuf, sbuf, lbuf, pbuf, recva, retbuf, inbuf, incs, incall, hid, ssq, sendb, recvb, acc, o2, osend,
    ylocal, gsil, expx_s,
    ins, wl_sem, ws, wr, as_, ar, bs, br, ds, dr, rs_s, rs_r,
):
    s = lax.axis_index("seq")
    h = lax.axis_index("head")
    k = s // 2
    c = lax.rem(s, 2)
    cx = k // NY
    cy = lax.rem(k, NY)
    sib = (k * 2 + 1 - c, h)

    def chip(a, b):
        return lax.rem(cx + a, NY) * NY + lax.rem(cy + b, NY)

    offs = [(a, b) for a in range(NY) for b in range(NY) if (a, b) != (0, 0)]
    offs.sort(key=lambda o: -(min(o[0], NY - o[0]) + min(o[1], NY - o[1])))
    hops = sorted({j - parent(j) for j in range(1, NZ // 2 + 1)})
    zs = [d for a in hops for d in (a, NZ - a)]

    loads = []
    for n, (src, dst) in enumerate((
        (ld_hbm, ld_ref), (dt_hbm, dt_ref), (x_hbm, x_ref), (b_hbm, b_ref), (c_hbm, c_ref),
        (skip_hbm, skip_ref), (z_hbm, z_ref), (gain_hbm, gain_ref),
    )):
        cp = pltpu.make_async_copy(src, dst, ins.at[n])
        cp.start()
        loads.append(cp)

    partners = [sib]
    partners += [(chip(a, b) * 2 + c, h) for a, b in offs]
    partners += [(s, lax.rem(h + d, NZ)) for d in zs]
    barrier = pltpu.get_barrier_semaphore()
    for p in partners:
        pl.semaphore_signal(barrier, inc=1, device_id=p, device_id_type=MESH)
    wl = pltpu.make_async_copy(w_ref, wbuf.at[k], wl_sem)
    wl.start()

    row = iota((128, 128), 0)
    col = iota((128, 128), 1)
    eye = (row == col).astype(F32)
    lower = row >= col
    loads[0].wait()
    loads[1].wait()
    ld = ld_ref[...]
    dt = dt_ref[...]
    sums3 = nt(split3(ld), lower.astype(BF16))
    run_r = sums3[0:8] + sums3[8:16] + sums3[16:24]
    heads = (iota((8, 512), 1) // 64 == iota((8, 512), 0)).astype(F32)
    heads4 = (iota((32, 512), 1) // 64 == lax.rem(iota((32, 512), 0), 8)).astype(BF16)

    def expand(v):
        return lax.dot_general(
            split3(v), heads4, (((0,), (0,)), ((), ())), preferred_element_type=F32
        )

    total_h = run_r[:, 127:128]
    tailx = expand(jnp.exp(total_h - run_r) * dt)
    total = jnp.sum(total_h * heads, axis=0, keepdims=True)
    loads[2].wait()
    xf = x_ref[...].astype(F32)
    xt = (xf * tailx).astype(BF16)
    loads[3].wait()
    keys = b_ref[...]
    state = lax.dot_general(keys, xt, (((0,), (0,)), ((), ())), preferred_element_type=F32)
    for hf in range(2):
        sbuf[hf, 0:128, :] = state[:, 256 * hf : 256 * hf + 256]
        sbuf[hf, 128:136, :] = jnp.broadcast_to(total[:, 256 * hf : 256 * hf + 256], (8, 256))

    pl.semaphore_wait(barrier, len(partners))

    def to_sib(src, dst, n):
        return pltpu.make_async_remote_copy(
            src_ref=src, dst_ref=dst, send_sem=ds.at[n], recv_sem=dr.at[n],
            device_id=sib, device_id_type=MESH,
        )

    swap = to_sib(sbuf.at[1 - c], lbuf, 0)
    swap.start()

    w_sent = []

    def w_copy(src, kk, half, dx, dy, dest):
        return pltpu.make_async_remote_copy(
            src_ref=src, dst_ref=wbuf.at[kk, pl.ds(256 * half, 256)],
            send_sem=ws.at[len(w_sent)], recv_sem=wr.at[half, NY * dx + dy],
            device_id=(dest * 2 + c, h), device_id_type=MESH,
        )

    def send_w(src, kk, half, dx, dy, dest):
        cp = w_copy(src, kk, half, dx, dy, dest)
        cp.start()
        w_sent.append(cp)

    def own_w(half):
        return w_ref.at[pl.ds(256 * half, 256)]

    def wait_w(half, kk, at):
        pltpu.make_async_remote_copy(
            src_ref=wbuf.at[kk, pl.ds(256 * half, 256)], dst_ref=wbuf.at[kk, pl.ds(256 * half, 256)],
            send_sem=ws.at[0], recv_sem=wr.at[half, at], device_id=sib, device_id_type=MESH,
        ).wait_recv()

    def pass_on(which):
        for d, half in which:
            if half == 0:
                kk = chip(0, NY - d)
                wait_w(0, kk, NY - d)
                for e in (2, 1, 3):
                    send_w(wbuf.at[kk, pl.ds(0, 256)], kk, 0, NY - e, NY - d, chip(e, 0))
            else:
                kk = chip(NY - d, 0)
                wait_w(1, kk, NY * (NY - d))
                for e in (2, 1, 3):
                    send_w(wbuf.at[kk, pl.ds(256, 256)], kk, 1, NY - d, NY - e, chip(0, e))

    for d in (2, 1, 3):
        send_w(own_w(0), k, 0, 0, NY - d, chip(0, d))
        send_w(own_w(1), k, 1, NY - d, 0, chip(d, 0))

    swap.wait()
    mine = sbuf[c]
    other = lbuf[...]
    early_own = jnp.full((1, 1), c, jnp.int32) == 0
    early = jnp.where(early_own, mine, other)
    later = jnp.where(early_own, other, mine)
    state_e = early[0:128]
    decay_e = early[128:129]
    decay_o = later[128:129]
    pair = (jnp.exp(decay_o) * state_e + later[0:128]).astype(BF16)
    decay_p = decay_e + decay_o
    hi = decay_p.astype(BF16).astype(F32)
    mid = (decay_p - hi).astype(BF16).astype(F32)
    low = decay_p - hi - mid
    r16 = iota((16, 256), 0)
    parts = jnp.where(r16 == 0, hi, jnp.where(r16 == 1, mid, jnp.where(r16 == 2, low, 0.0)))
    parts = parts.astype(BF16)
    for q in range(NCHIP):
        n0, l0 = 16 * (q % 8), 128 * (q // 8)
        pbuf[q, 0:16, :] = pair[n0 : n0 + 16, l0 : l0 + 128]
        pbuf[q, 16:32, :] = parts[:, l0 : l0 + 128]
    to_owner = []
    for n, (a, b) in enumerate(offs):
        q = chip(a, b)
        cp = pltpu.make_async_remote_copy(
            src_ref=pbuf.at[q, pl.ds(0, 24)], dst_ref=recva.at[k, pl.ds(0, 24)], send_sem=as_.at[n], recv_sem=ar.at[n],
            device_id=(q * 2 + c, h), device_id_type=MESH,
        )
        cp.start()
        to_owner.append(cp)
    recva[k, 0:24] = pbuf[k, 0:24]
    for d in (2, 1, 3):
        send_w(own_w(0), k, 0, NY - d, 0, chip(d, 0))
        send_w(own_w(1), k, 1, 0, NY - d, chip(0, d))

    for cp in loads[4:]:
        cp.wait()
    queries = c_ref[...]
    skip = jnp.dot(skip_ref[...], heads, precision=HIGH, preferred_element_type=F32)
    scores = nt(queries, keys)
    lane = iota((128, 128), 1)
    run_c = nt(lower.astype(F32), ld, HIGH)
    expx_s[...] = expand(jnp.exp(run_r))
    for p in range(4):
        xp = x_ref[:, 128 * p : 128 * p + 128]
        ys = []
        for hh in (2 * p, 2 * p + 1):
            spread = run_c[:, hh : hh + 1] - run_r[hh : hh + 1, :]
            m = jnp.exp(jnp.where(lower, spread, -1e30)) * (scores * dt[hh : hh + 1, :])
            ys.append(jnp.dot(m.astype(BF16), xp, preferred_element_type=F32))
        ylocal[:, 128 * p : 128 * p + 128] = (
            jnp.where(lane < 64, ys[0], ys[1])
            + skip[:, 128 * p : 128 * p + 128] * xp.astype(F32)
        )
    zf = z_ref[...].astype(F32)
    gsil[...] = zf / (1.0 + jnp.exp(-zf))

    for cp in to_owner:
        cp.wait_recv()
    carry = jnp.zeros((16, 128), F32)
    for kk in range(NCHIP):
        retbuf[kk] = carry.astype(BF16)
        m = recva[kk, 0:24].astype(F32)
        carry = jnp.exp(m[16:17] + m[17:18] + m[18:19]) * carry + m[0:16]
    back = []
    for n, (a, b) in enumerate(offs):
        q = chip(a, b)
        cp = pltpu.make_async_remote_copy(
            src_ref=retbuf.at[q], dst_ref=inbuf.at[k], send_sem=bs.at[n], recv_sem=br.at[n],
            device_id=(q * 2 + c, h), device_id_type=MESH,
        )
        cp.start()
        back.append(cp)
    inbuf[k] = retbuf[k]
    pass_on(PASSED)
    wl.wait()

    for cp in back:
        cp.wait_recv()
    incoming = jnp.concatenate(
        [inbuf[8 * i : 8 * i + 8].reshape(128, 128).astype(F32) for i in range(2)], axis=1
    )
    inc_odd = jnp.exp(decay_e) * incoming + state_e
    incs[...] = jnp.where(early_own, inc_odd, incoming).astype(BF16)
    swap2 = to_sib(incs, incall.at[c], 1)
    swap2.start()
    incall[c] = jnp.where(early_own, incoming, inc_odd).astype(BF16)
    swap2.wait()

    gain = gain_ref[...]
    for hf in range(2):
        l0 = 256 * hf
        carried = jnp.dot(queries, incall[hf], preferred_element_type=F32)
        y = ylocal[:, l0 : l0 + 256] + carried * expx_s[:, l0 : l0 + 256]
        g = y * gsil[:, l0 : l0 + 256]
        square = g * g if hf == 0 else square + g * g
        hid[c, :, l0 : l0 + 256] = (g * gain[:, l0 : l0 + 256]).astype(BF16)
    swap3 = to_sib(hid.at[c], hid.at[c], 2)
    swap3.start()
    ssq[c] = nt(jnp.ones((8, 256), F32), square, HIGH)
    swap4 = to_sib(ssq.at[c], ssq.at[c], 3)
    swap4.start()
    swap3.wait()
    swap4.wait()

    sides = {0: 8, 1: 7}
    slot = {}
    for side, most in sides.items():
        for j in range(1, most + 1):
            slot[side, j] = len(slot)
    halves = (1 - c, c)
    own_sq = [ssq[t, 0:1, :] for t in halves]
    r16 = iota((16, 128), 0)

    def target(side, j):
        return lax.rem(h + (NZ - j if side == 0 else j), NZ)

    def split_sq(sq):
        ext = jnp.zeros((16, 128), F32)
        for t, v in enumerate(sq):
            top = v.astype(BF16).astype(F32)
            ext = jnp.where(r16 == 2 * t, top, jnp.where(r16 == 2 * t + 1, v - top, ext))
        return ext.astype(BF16)

    own_ext = split_sq(own_sq)
    sent = {}

    def send(side, j, t):
        n = slot[side, j]
        rows = pl.ds(0, 128 if t else 136)
        cp = pltpu.make_async_remote_copy(
            src_ref=sendb.at[n, t, rows], dst_ref=recvb.at[n, t, rows],
            send_sem=rs_s.at[n, t], recv_sem=rs_r.at[n, t],
            device_id=(s, target(side, j - parent(j))), device_id_type=MESH,
        )
        cp.start()
        sent[side, j, t] = cp

    def project(dest):
        at = lax.rem(dest // NY - cx + NY, NY) * NY + lax.rem(lax.rem(dest, NY) - cy + NY, NY)

        for half in (0, 1):
            @pl.when(at >= NY if half == 0 else lax.rem(at, NY) > 0)
            def _(half=half):
                wait_w(half, dest, at)

        wb = wbuf[dest]
        return [jnp.dot(hid[t], wb, preferred_element_type=F32) for t in halves]

    def leaf(side, j):
        n = slot[side, j]
        for t, part in enumerate(project(target(side, j))):
            sendb[n, t, 0:128, :] = part.astype(BF16)
        sendb[n, 0, 128:144, :] = own_ext

    def prepare(n, dest):
        for t, part in enumerate(project(dest)):
            acc[n, t] = part

    def gather(n, t, kids):
        part = acc[n, t]
        sq = list(own_sq)
        for side, i in kids:
            sent[side, i, t].wait_recv()
            got = recvb[slot[side, i], t].astype(F32)
            part = part + got[0:128]
            for u in (0, 1):
                sq[u] = sq[u] + got[128 + 2 * u : 129 + 2 * u] + got[129 + 2 * u : 130 + 2 * u]
        return part, sq

    def relay(side, j, t):
        kids = [(side, i) for i in range(j + 1, sides[side] + 1) if parent(i) == j]
        part, sq = gather(RELAYS.index(j) * 2 + side, t, kids)
        n = slot[side, j]
        sendb[n, t, 0:128, :] = part.astype(BF16)
        if t == 0:
            sendb[n, 0, 128:144, :] = split_sq(sq)
        send(side, j, t)

    both = (0, 1)
    for step in ORDER:
        kind, j, t = step[0], int(step[1]), int(step[2:] or 0)
        if j == 0:
            prepare(2 * len(RELAYS), h)
            continue
        for side in both:
            if (side, j) not in slot:
                continue
            if kind == "P":
                prepare(RELAYS.index(j) * 2 + side, target(side, j))
            elif kind == "R":
                relay(side, j, t)
            else:
                if kind in "LX":
                    leaf(side, j)
                if kind in "SX":
                    send(side, j, t)

    last = [(side, i) for side in both for i in range(1, 9) if (side, i) in slot and parent(i) == 0]
    for t in (0, 1):
        part, sq = gather(2 * len(RELAYS), t, last)
        if t == 0:
            scale = [lax.rsqrt(v * (1.0 / 8192.0) + 1e-05) for v in sq]
            scale = [jnp.broadcast_to(v, (8, 128)).T[:, 0:1] for v in scale]
        done = (part * scale[t]).astype(BF16)
        if t == 0:
            osend[...] = done
            swap5 = to_sib(osend, o2.at[c], 4)
            swap5.start()
        else:
            o2[c] = done
    for cp in w_sent + to_owner + back + list(sent.values()):
        cp.wait_send()
    swap5.wait()
    out_ref[:, 0:128] = o2[0]
    out_ref[:, 128:256] = o2[1]


def body(
    signal, gate_input, state_in, state_out, step_size, log_decay, skip_gain, norm_gain, out_weight
):
    vmem = pl.BlockSpec(memory_space=pltpu.VMEM)
    args = [pltpu.with_memory_space_constraint(a, pltpu.HBM) for a in (
        signal, gate_input, state_in, state_out, step_size, log_decay,
        skip_gain.reshape(1, -1), norm_gain.reshape(1, -1), out_weight,
    )]
    dma = pltpu.SemaphoreType.DMA
    return pl.pallas_call(
        kernel,
        out_shape=jax.ShapeDtypeStruct((128, 256), BF16),
        in_specs=[pl.BlockSpec(memory_space=pltpu.HBM)] * 9,
        out_specs=vmem,
        scratch_shapes=[
            pltpu.VMEM((128, 512), BF16),
            pltpu.VMEM((128, 512), BF16),
            pltpu.VMEM((128, 128), BF16),
            pltpu.VMEM((128, 128), BF16),
            pltpu.VMEM((8, 128), F32),
            pltpu.VMEM((8, 128), F32),
            pltpu.VMEM((1, 8), F32),
            pltpu.VMEM((1, 512), F32),
            pltpu.VMEM((NCHIP, 512, 128), BF16),
            pltpu.VMEM((2, 136, 256), F32),
            pltpu.VMEM((136, 256), F32),
            pltpu.VMEM((NCHIP, 32, 128), BF16),
            pltpu.VMEM((NCHIP, 32, 128), BF16),
            pltpu.VMEM((NCHIP, 16, 128), BF16),
            pltpu.VMEM((NCHIP, 16, 128), BF16),
            pltpu.VMEM((128, 256), BF16),
            pltpu.VMEM((2, 128, 256), BF16),
            pltpu.VMEM((2, 128, 512), BF16),
            pltpu.VMEM((2, 8, 128), F32),
            pltpu.VMEM((15, 2, 144, 128), BF16),
            pltpu.VMEM((15, 2, 144, 128), BF16),
            pltpu.VMEM((7, 2, 128, 128), F32),
            pltpu.VMEM((2, 128, 128), BF16),
            pltpu.VMEM((128, 128), BF16),
            pltpu.VMEM((128, 512), F32),
            pltpu.VMEM((128, 512), F32),
            pltpu.VMEM((128, 512), F32),
            dma((8,)),
            dma,
            dma((30,)), dma((2, 16)),
            dma((15,)), dma((15,)),
            dma((15,)), dma((15,)),
            dma((5,)), dma((5,)),
            dma((15, 2)), dma((15, 2)),
        ],
        compiler_params=pltpu.CompilerParams(
            collective_id=0, has_side_effects=True, vmem_limit_bytes=40 * 2**20
        ),
        name="ssd_layer",
    )(*args)


def solution(mesh):
    in_specs = (
        P("seq", "head"),
        P("seq", "head"),
        P("seq", None),
        P("seq", None),
        P("head", "seq"),
        P("head", "seq"),
        P("head"),
        P("head"),
        P("head", "seq"),
    )
    out_specs = P("seq", "head")
    return jax.shard_map(body, mesh=mesh, in_specs=in_specs, out_specs=out_specs, check_vma=False)
```

```python
import jax
import jax.numpy as jnp
from jax import lax
from jax.experimental import pallas as pl
from jax.experimental.pallas import tpu as pltpu
from jax.sharding import PartitionSpec as P

MESH = pl.DeviceIdType.MESH
HIGH = lax.Precision.HIGHEST
F32 = jnp.float32
BF16 = jnp.bfloat16
NY = 4
NCHIP = 16
PASSED = ((1, 0), (1, 1), (3, 0), (3, 1), (2, 0), (2, 1))
NZ = 16
RELAYS = (2, 4, 6)
ORDER = (
    "X8", "X7", "S81", "S71", "X5", "P6", "R60", "S51",
    "R61", "X3", "P4", "R40", "S31", "R41", "X1", "P2",
    "R20", "S11", "R21", "P0",
)


def nt(a, b, precision=None):
    return lax.dot_general(
        a, b, (((1,), (1,)), ((), ())), precision=precision, preferred_element_type=F32
    )


def split3(v):
    hi = v.astype(BF16).astype(F32)
    mid = (v - hi).astype(BF16).astype(F32)
    return jnp.concatenate([hi, mid, v - hi - mid, jnp.zeros_like(v)], axis=0).astype(BF16)


def parent(j):
    return max(r for r in (0,) + RELAYS if r < j)


def iota(shape, dim):
    return lax.broadcasted_iota(jnp.int32, shape, dim)


def kernel(
    x_hbm, z_hbm, b_hbm, c_hbm, dt_hbm, ld_hbm, skip_hbm, gain_hbm, w_ref,
    out_ref,
    x_ref, z_ref, b_ref, c_ref, dt_ref, ld_ref, skip_ref, gain_ref,
    wbuf, sbuf, lbuf, pbuf, recva, retbuf, inbuf, incs, incall, hid, ssq, sendb, recvb, acc, o2, osend,
    ylocal, gsil, expx_s,
    ins, wl_sem, ws, wr, as_, ar, bs, br, ds, dr, rs_s, rs_r,
):
    s = lax.axis_index("seq")
    h = lax.axis_index("head")
    k = s // 2
    c = lax.rem(s, 2)
    cx = k // NY
    cy = lax.rem(k, NY)
    sib = (k * 2 + 1 - c, h)

    def chip(a, b):
        return lax.rem(cx + a, NY) * NY + lax.rem(cy + b, NY)

    offs = [(a, b) for a in range(NY) for b in range(NY) if (a, b) != (0, 0)]
    offs.sort(key=lambda o: -(min(o[0], NY - o[0]) + min(o[1], NY - o[1])))
    hops = sorted({j - parent(j) for j in range(1, NZ // 2 + 1)})
    zs = [d for a in hops for d in (a, NZ - a)]

    loads = []
    for n, (src, dst) in enumerate((
        (ld_hbm, ld_ref), (dt_hbm, dt_ref), (x_hbm, x_ref), (b_hbm, b_ref), (c_hbm, c_ref),
        (skip_hbm, skip_ref), (z_hbm, z_ref), (gain_hbm, gain_ref),
    )):
        cp = pltpu.make_async_copy(src, dst, ins.at[n])
        cp.start()
        loads.append(cp)

    partners = [sib]
    partners += [(chip(a, b) * 2 + c, h) for a, b in offs]
    partners += [(s, lax.rem(h + d, NZ)) for d in zs]
    barrier = pltpu.get_barrier_semaphore()
    for p in partners:
        pl.semaphore_signal(barrier, inc=1, device_id=p, device_id_type=MESH)
    wl = pltpu.make_async_copy(w_ref, wbuf.at[k], wl_sem)
    wl.start()

    row = iota((128, 128), 0)
    col = iota((128, 128), 1)
    eye = (row == col).astype(F32)
    lower = row >= col
    loads[0].wait()
    loads[1].wait()
    ld = ld_ref[...]
    dt = dt_ref[...]
    sums3 = nt(split3(ld), lower.astype(BF16))
    run_r = sums3[0:8] + sums3[8:16] + sums3[16:24]
    heads = (iota((8, 512), 1) // 64 == iota((8, 512), 0)).astype(F32)
    heads4 = (iota((32, 512), 1) // 64 == lax.rem(iota((32, 512), 0), 8)).astype(BF16)

    def expand(v):
        return lax.dot_general(
            split3(v), heads4, (((0,), (0,)), ((), ())), preferred_element_type=F32
        )

    total_h = run_r[:, 127:128]
    tailx = expand(jnp.exp(total_h - run_r) * dt)
    total = jnp.sum(total_h * heads, axis=0, keepdims=True)
    loads[2].wait()
    xf = x_ref[...].astype(F32)
    xt = (xf * tailx).astype(BF16)
    loads[3].wait()
    keys = b_ref[...]
    state = lax.dot_general(keys, xt, (((0,), (0,)), ((), ())), preferred_element_type=F32)
    for hf in range(2):
        sbuf[hf, 0:128, :] = state[:, 256 * hf : 256 * hf + 256]
        sbuf[hf, 128:136, :] = jnp.broadcast_to(total[:, 256 * hf : 256 * hf + 256], (8, 256))

    pl.semaphore_wait(barrier, len(partners))

    def to_sib(src, dst, n):
        return pltpu.make_async_remote_copy(
            src_ref=src, dst_ref=dst, send_sem=ds.at[n], recv_sem=dr.at[n],
            device_id=sib, device_id_type=MESH,
        )

    swap = to_sib(sbuf.at[1 - c], lbuf, 0)
    swap.start()

    w_sent = []

    def w_copy(src, kk, half, dx, dy, dest):
        return pltpu.make_async_remote_copy(
            src_ref=src, dst_ref=wbuf.at[kk, pl.ds(256 * half, 256)],
            send_sem=ws.at[len(w_sent)], recv_sem=wr.at[half, NY * dx + dy],
            device_id=(dest * 2 + c, h), device_id_type=MESH,
        )

    def send_w(src, kk, half, dx, dy, dest):
        cp = w_copy(src, kk, half, dx, dy, dest)
        cp.start()
        w_sent.append(cp)

    def own_w(half):
        return w_ref.at[pl.ds(256 * half, 256)]

    def wait_w(half, kk, at):
        pltpu.make_async_remote_copy(
            src_ref=wbuf.at[kk, pl.ds(256 * half, 256)], dst_ref=wbuf.at[kk, pl.ds(256 * half, 256)],
            send_sem=ws.at[0], recv_sem=wr.at[half, at], device_id=sib, device_id_type=MESH,
        ).wait_recv()

    def pass_on(which):
        for d, half in which:
            if half == 0:
                kk = chip(0, NY - d)
                wait_w(0, kk, NY - d)
                for e in (2, 1, 3):
                    send_w(wbuf.at[kk, pl.ds(0, 256)], kk, 0, NY - e, NY - d, chip(e, 0))
            else:
                kk = chip(NY - d, 0)
                wait_w(1, kk, NY * (NY - d))
                for e in (2, 1, 3):
                    send_w(wbuf.at[kk, pl.ds(256, 256)], kk, 1, NY - d, NY - e, chip(0, e))

    for d in (2, 1, 3):
        send_w(own_w(0), k, 0, 0, NY - d, chip(0, d))
        send_w(own_w(1), k, 1, NY - d, 0, chip(d, 0))

    swap.wait()
    mine = sbuf[c]
    other = lbuf[...]
    early_own = jnp.full((1, 1), c, jnp.int32) == 0
    early = jnp.where(early_own, mine, other)
    later = jnp.where(early_own, other, mine)
    state_e = early[0:128]
    decay_e = early[128:129]
    decay_o = later[128:129]
    pair = (jnp.exp(decay_o) * state_e + later[0:128]).astype(BF16)
    decay_p = decay_e + decay_o
    hi = decay_p.astype(BF16).astype(F32)
    mid = (decay_p - hi).astype(BF16).astype(F32)
    low = decay_p - hi - mid
    r16 = iota((16, 256), 0)
    parts = jnp.where(r16 == 0, hi, jnp.where(r16 == 1, mid, jnp.where(r16 == 2, low, 0.0)))
    parts = parts.astype(BF16)
    for q in range(NCHIP):
        n0, l0 = 16 * (q % 8), 128 * (q // 8)
        pbuf[q, 0:16, :] = pair[n0 : n0 + 16, l0 : l0 + 128]
        pbuf[q, 16:32, :] = parts[:, l0 : l0 + 128]
    to_owner = []
    for n, (a, b) in enumerate(offs):
        q = chip(a, b)
        cp = pltpu.make_async_remote_copy(
            src_ref=pbuf.at[q, pl.ds(0, 24)], dst_ref=recva.at[k, pl.ds(0, 24)], send_sem=as_.at[n], recv_sem=ar.at[n],
            device_id=(q * 2 + c, h), device_id_type=MESH,
        )
        cp.start()
        to_owner.append(cp)
    recva[k, 0:24] = pbuf[k, 0:24]
    wl.wait()
    for d in (2, 1, 3):
        send_w(wbuf.at[k, pl.ds(0, 256)], k, 0, NY - d, 0, chip(d, 0))
        send_w(wbuf.at[k, pl.ds(256, 256)], k, 1, 0, NY - d, chip(0, d))

    for cp in loads[4:]:
        cp.wait()
    queries = c_ref[...]
    skip = jnp.dot(skip_ref[...], heads, precision=HIGH, preferred_element_type=F32)
    scores = nt(queries, keys)
    lane = iota((128, 128), 1)
    run_c = nt(lower.astype(F32), ld, HIGH)
    expx_s[...] = expand(jnp.exp(run_r))
    for p in range(4):
        xp = x_ref[:, 128 * p : 128 * p + 128]
        ys = []
        for hh in (2 * p, 2 * p + 1):
            spread = run_c[:, hh : hh + 1] - run_r[hh : hh + 1, :]
            m = jnp.exp(jnp.where(lower, spread, -1e30)) * (scores * dt[hh : hh + 1, :])
            ys.append(jnp.dot(m.astype(BF16), xp, preferred_element_type=F32))
        ylocal[:, 128 * p : 128 * p + 128] = (
            jnp.where(lane < 64, ys[0], ys[1])
            + skip[:, 128 * p : 128 * p + 128] * xp.astype(F32)
        )
    zf = z_ref[...].astype(F32)
    gsil[...] = zf / (1.0 + jnp.exp(-zf))

    for cp in to_owner:
        cp.wait_recv()
    carry = jnp.zeros((16, 128), F32)
    for kk in range(NCHIP):
        retbuf[kk] = carry.astype(BF16)
        m = recva[kk, 0:24].astype(F32)
        carry = jnp.exp(m[16:17] + m[17:18] + m[18:19]) * carry + m[0:16]
    back = []
    for n, (a, b) in enumerate(offs):
        q = chip(a, b)
        cp = pltpu.make_async_remote_copy(
            src_ref=retbuf.at[q], dst_ref=inbuf.at[k], send_sem=bs.at[n], recv_sem=br.at[n],
            device_id=(q * 2 + c, h), device_id_type=MESH,
        )
        cp.start()
        back.append(cp)
    inbuf[k] = retbuf[k]
    pass_on(PASSED)

    for cp in back:
        cp.wait_recv()
    incoming = jnp.concatenate(
        [inbuf[8 * i : 8 * i + 8].reshape(128, 128).astype(F32) for i in range(2)], axis=1
    )
    inc_odd = jnp.exp(decay_e) * incoming + state_e
    incs[...] = jnp.where(early_own, inc_odd, incoming).astype(BF16)
    swap2 = to_sib(incs, incall.at[c], 1)
    swap2.start()
    incall[c] = jnp.where(early_own, incoming, inc_odd).astype(BF16)
    swap2.wait()

    gain = gain_ref[...]
    for hf in range(2):
        l0 = 256 * hf
        carried = jnp.dot(queries, incall[hf], preferred_element_type=F32)
        y = ylocal[:, l0 : l0 + 256] + carried * expx_s[:, l0 : l0 + 256]
        g = y * gsil[:, l0 : l0 + 256]
        square = g * g if hf == 0 else square + g * g
        hid[c, :, l0 : l0 + 256] = (g * gain[:, l0 : l0 + 256]).astype(BF16)
    swap3 = to_sib(hid.at[c], hid.at[c], 2)
    swap3.start()
    ssq[c] = nt(jnp.ones((8, 256), F32), square, HIGH)
    swap4 = to_sib(ssq.at[c], ssq.at[c], 3)
    swap4.start()
    swap3.wait()
    swap4.wait()

    sides = {0: 8, 1: 7}
    slot = {}
    for side, most in sides.items():
        for j in range(1, most + 1):
            slot[side, j] = len(slot)
    halves = (1 - c, c)
    own_sq = [ssq[t, 0:1, :] for t in halves]
    r16 = iota((16, 128), 0)

    def target(side, j):
        return lax.rem(h + (NZ - j if side == 0 else j), NZ)

    def split_sq(sq):
        ext = jnp.zeros((16, 128), F32)
        for t, v in enumerate(sq):
            top = v.astype(BF16).astype(F32)
            ext = jnp.where(r16 == 2 * t, top, jnp.where(r16 == 2 * t + 1, v - top, ext))
        return ext.astype(BF16)

    own_ext = split_sq(own_sq)
    sent = {}

    def send(side, j, t):
        n = slot[side, j]
        rows = pl.ds(0, 128 if t else 136)
        cp = pltpu.make_async_remote_copy(
            src_ref=sendb.at[n, t, rows], dst_ref=recvb.at[n, t, rows],
            send_sem=rs_s.at[n, t], recv_sem=rs_r.at[n, t],
            device_id=(s, target(side, j - parent(j))), device_id_type=MESH,
        )
        cp.start()
        sent[side, j, t] = cp

    def project(dest):
        at = lax.rem(dest // NY - cx + NY, NY) * NY + lax.rem(lax.rem(dest, NY) - cy + NY, NY)

        for half in (0, 1):
            @pl.when(at >= NY if half == 0 else lax.rem(at, NY) > 0)
            def _(half=half):
                wait_w(half, dest, at)

        wb = wbuf[dest]
        return [jnp.dot(hid[t], wb, preferred_element_type=F32) for t in halves]

    def leaf(side, j):
        n = slot[side, j]
        for t, part in enumerate(project(target(side, j))):
            sendb[n, t, 0:128, :] = part.astype(BF16)
        sendb[n, 0, 128:144, :] = own_ext

    def prepare(n, dest):
        for t, part in enumerate(project(dest)):
            acc[n, t] = part

    def gather(n, t, kids):
        part = acc[n, t]
        sq = list(own_sq)
        for side, i in kids:
            sent[side, i, t].wait_recv()
            got = recvb[slot[side, i], t].astype(F32)
            part = part + got[0:128]
            for u in (0, 1):
                sq[u] = sq[u] + got[128 + 2 * u : 129 + 2 * u] + got[129 + 2 * u : 130 + 2 * u]
        return part, sq

    def relay(side, j, t):
        kids = [(side, i) for i in range(j + 1, sides[side] + 1) if parent(i) == j]
        part, sq = gather(RELAYS.index(j) * 2 + side, t, kids)
        n = slot[side, j]
        sendb[n, t, 0:128, :] = part.astype(BF16)
        if t == 0:
            sendb[n, 0, 128:144, :] = split_sq(sq)
        send(side, j, t)

    both = (0, 1)
    for step in ORDER:
        kind, j, t = step[0], int(step[1]), int(step[2:] or 0)
        if j == 0:
            prepare(2 * len(RELAYS), h)
            continue
        for side in both:
            if (side, j) not in slot:
                continue
            if kind == "P":
                prepare(RELAYS.index(j) * 2 + side, target(side, j))
            elif kind == "R":
                relay(side, j, t)
            else:
                if kind in "LX":
                    leaf(side, j)
                if kind in "SX":
                    send(side, j, t)

    last = [(side, i) for side in both for i in range(1, 9) if (side, i) in slot and parent(i) == 0]
    for t in (0, 1):
        part, sq = gather(2 * len(RELAYS), t, last)
        if t == 0:
            scale = [lax.rsqrt(v * (1.0 / 8192.0) + 1e-05) for v in sq]
            scale = [jnp.broadcast_to(v, (8, 128)).T[:, 0:1] for v in scale]
        done = (part * scale[t]).astype(BF16)
        if t == 0:
            osend[...] = done
            swap5 = to_sib(osend, o2.at[c], 4)
            swap5.start()
        else:
            o2[c] = done
    for cp in w_sent + to_owner + back + list(sent.values()):
        cp.wait_send()
    swap5.wait()
    out_ref[:, 0:128] = o2[0]
    out_ref[:, 128:256] = o2[1]


def body(
    signal, gate_input, state_in, state_out, step_size, log_decay, skip_gain, norm_gain, out_weight
):
    vmem = pl.BlockSpec(memory_space=pltpu.VMEM)
    args = [pltpu.with_memory_space_constraint(a, pltpu.HBM) for a in (
        signal, gate_input, state_in, state_out, step_size, log_decay,
        skip_gain.reshape(1, -1), norm_gain.reshape(1, -1), out_weight,
    )]
    dma = pltpu.SemaphoreType.DMA
    return pl.pallas_call(
        kernel,
        out_shape=jax.ShapeDtypeStruct((128, 256), BF16),
        in_specs=[pl.BlockSpec(memory_space=pltpu.HBM)] * 9,
        out_specs=vmem,
        scratch_shapes=[
            pltpu.VMEM((128, 512), BF16),
            pltpu.VMEM((128, 512), BF16),
            pltpu.VMEM((128, 128), BF16),
            pltpu.VMEM((128, 128), BF16),
            pltpu.VMEM((8, 128), F32),
            pltpu.VMEM((8, 128), F32),
            pltpu.VMEM((1, 8), F32),
            pltpu.VMEM((1, 512), F32),
            pltpu.VMEM((NCHIP, 512, 128), BF16),
            pltpu.VMEM((2, 136, 256), F32),
            pltpu.VMEM((136, 256), F32),
            pltpu.VMEM((NCHIP, 32, 128), BF16),
            pltpu.VMEM((NCHIP, 32, 128), BF16),
            pltpu.VMEM((NCHIP, 16, 128), BF16),
            pltpu.VMEM((NCHIP, 16, 128), BF16),
            pltpu.VMEM((128, 256), BF16),
            pltpu.VMEM((2, 128, 256), BF16),
            pltpu.VMEM((2, 128, 512), BF16),
            pltpu.VMEM((2, 8, 128), F32),
            pltpu.VMEM((15, 2, 144, 128), BF16),
            pltpu.VMEM((15, 2, 144, 128), BF16),
            pltpu.VMEM((7, 2, 128, 128), F32),
            pltpu.VMEM((2, 128, 128), BF16),
            pltpu.VMEM((128, 128), BF16),
            pltpu.VMEM((128, 512), F32),
            pltpu.VMEM((128, 512), F32),
            pltpu.VMEM((128, 512), F32),
            dma((8,)),
            dma,
            dma((30,)), dma((2, 16)),
            dma((15,)), dma((15,)),
            dma((15,)), dma((15,)),
            dma((5,)), dma((5,)),
            dma((15, 2)), dma((15, 2)),
        ],
        compiler_params=pltpu.CompilerParams(
            collective_id=0, has_side_effects=True, vmem_limit_bytes=40 * 2**20
        ),
        name="ssd_layer",
    )(*args)


def solution(mesh):
    in_specs = (
        P("seq", "head"),
        P("seq", "head"),
        P("seq", None),
        P("seq", None),
        P("head", "seq"),
        P("head", "seq"),
        P("head"),
        P("head"),
        P("head", "seq"),
    )
    out_specs = P("seq", "head")
    return jax.shard_map(body, mesh=mesh, in_specs=in_specs, out_specs=out_specs, check_vma=False)
```
